256 devices in a mesh: expert: 64 (over y, z, core), tensor: 4 (over x).
Axes of the slice: x: 4, y: 4, z: 8, core: 2. Of those that a mesh axis runs over, the one named last changes fastest.
Arguments:
- tokens: bfloat16 [4096, 7168], P(('expert', 'tensor')), may hold values from -6 to 6
- expert_ids: int32 [4096, 8], P(('expert', 'tensor')), may hold values from 0 to 63, all different within a row; in each aligned block of 16 rows (0 to 15, 16 to 31, ...) at most 4 rows name the same one
- gate_values: float32 [4096, 8], P(('expert', 'tensor')), may hold values from 0.05 to 0.6
- w_gate: bfloat16 [64, 7168, 1024], P('expert', None, 'tensor'), may hold values from -0.0625 to 0.0625
- w_up: bfloat16 [64, 7168, 1024], P('expert', None, 'tensor'), may hold values from -0.0625 to 0.0625
- w_down: bfloat16 [64, 1024, 7168], P('expert', 'tensor'), may hold values from -0.1875 to 0.1875
Outputs:
- mixed: bfloat16 [4096, 7168], P(('expert', 'tensor'))
The draws below stay inside these ranges and needn't reach their ends.
Inputs may be any that keep to these rules, and one draw needn't show every extreme that they name: `expert_ids`: each row names 8 different experts; within each aligned block of 16 rows (the rows of one device) no expert is named by more than 4 rows.
All inputs are finite; a program needn't handle non-finite values.
Results may differ from the reference program's by a relative error of at most 0.012.
Values may be sent and summed in bfloat16 or wider, within the bound.
A program may use at most 128 MiB of HBM per device.

```python
import math
import jax
import jax.numpy as jnp
import numpy as np
from jax import lax

D = 7168
FF = 1024
TOP = 8
TOK_DEV = 16
EXPERTS = 64
CAP = 4
TOKENS = 4096
N_TENSOR = 4


def levels(rng, dims, cuts, smallest, largest):
    factor_of, own = 1.0, jax.random.fold_in(rng, 6)
    for axis_at, blocks in cuts:
        steps = jnp.exp(jax.random.uniform(jax.random.fold_in(own, axis_at), (blocks,), jnp.float32, smallest / len(cuts), largest / len(cuts)))
        factor_of = factor_of * jnp.repeat(steps, dims[axis_at] // blocks).reshape([-1 if axis == axis_at else 1 for axis in range(len(dims))])
    return factor_of


def shared_out(stream_key, own, number, rows, amount, top, limit, lean):
    sequence = jax.random.permutation(stream_key, amount)
    heavy_load, ordinary = shares(amount, rows * top, limit, lean, True), shares(amount, rows * top, limit, lean, False)
    places = jnp.arange(amount)

    def named(sizes, turn):
        used = int((sizes > 0).sum())
        fixed = max(1, used // 4)
        moved = fixed + (places - fixed + turn * (used - fixed)) % max(1, amount - fixed)
        return jnp.zeros((amount,), jnp.int32).at[sequence[jnp.where(places < fixed, places, moved)]].set(jnp.asarray(sizes, jnp.int32))

    sizes = jnp.where(number % 4 == 0, named(heavy_load, number // 4), named(ordinary, number - number // 4 - 1))
    mixed = jax.random.permutation(jax.random.fold_in(own, 3), amount)
    source_of, sink = mixed[0:amount // 2 * 2:2], mixed[1:amount // 2 * 2:2]
    slack = jnp.minimum(sizes[source_of] - 1, limit - sizes[sink]) // 2
    slack = jnp.where((source_of == sequence[0]) | (sink == sequence[0]) | (sizes[sink] == 0), 0, jnp.maximum(slack, 0))
    moved = jax.random.randint(jax.random.fold_in(own, 4), (amount // 2,), 0, 1 << 20) % (slack + 1)
    sizes = sizes.at[source_of].add(-moved).at[sink].add(moved)
    members = jnp.searchsorted(jnp.cumsum(sizes), jnp.arange(rows * top), side="right").astype(jnp.int32)
    listing = members.reshape(top, rows).T
    listing = listing[jax.random.permutation(jax.random.fold_in(own, 1), rows)]
    turn = jax.random.randint(jax.random.fold_in(own, 2), (rows, 1), 0, top)
    return jnp.take_along_axis(listing, (jnp.arange(top)[None, :] + turn) % top, axis=1)


def shares(count, total, most, lean, full):
    loads = [(1 << 20) // math.isqrt(rank ** lean) + 1 for rank in range(1, count + 1)]
    largest = most if full else min(most, max(-(-total // count), total * loads[0] // sum(loads)))
    least = 1 if total - largest >= count - 1 else 0
    counts, spare = [largest] + [least] * (count - 1), total - largest - least * (count - 1)
    while spare > 0:
        free = [i for i in range(1, count) if counts[i] < largest] or [i for i in range(1, count) if counts[i] < most]
        mass, budget = sum([loads[i] for i in free]), spare
        for i in free:
            more = min(most - counts[i], max(1, budget * loads[i] // mass), spare)
            counts[i] = counts[i] + more
            spare = spare - more
    return np.array(counts)


def gaussian(own_key, extent, deviation, most, cuts=(), kind=jnp.bfloat16):
    entries = jax.random.normal(own_key, extent, jnp.float32) * deviation
    if len(cuts) > 0:
        entries = levels(own_key, extent, cuts, -0.22, 0.18) * entries
    return jnp.clip(entries, min=-most, max=most).astype(kind)


def setup_inputs(seed: int = 0) -> dict:
    key_of = jax.random.split(jax.random.key(seed), 7)
    tokens = gaussian(key_of[0], (TOKENS, D), 1.0, 6.0, ((0, 256),))
    expert_ids_keys = jax.random.split(jax.random.fold_in(key_of[1], 1), TOKENS // TOK_DEV)
    expert_ids_turns = jax.random.permutation(jax.random.fold_in(key_of[1], 3), TOKENS // TOK_DEV)
    expert_ids = jax.vmap(lambda own, number: shared_out(jax.random.fold_in(key_of[1], 2), own, number, TOK_DEV, EXPERTS, TOP, CAP, 2))(expert_ids_keys, expert_ids_turns).reshape((TOKENS, TOP))
    gate_values = jnp.clip(0.05 + 0.55 * jax.random.uniform(key_of[2], (TOKENS, TOP), jnp.float32) ** levels(key_of[2], (TOKENS, TOP), ((0, 256),), -0.2, 0.2), 0.05, 0.6)
    w_gate = gaussian(key_of[3], (EXPERTS, D, FF), D ** -0.5, 0.0625, ((0, 64), (2, 4)))
    w_up = gaussian(key_of[4], (EXPERTS, D, FF), D ** -0.5, 0.0625, ((0, 64), (2, 4)))
    w_down = gaussian(key_of[5], (EXPERTS, FF, D), FF ** -0.5, 0.1875, ((0, 64), (1, 4)))
    return {"tokens": tokens, "expert_ids": expert_ids, "gate_values": gate_values, "w_gate": w_gate, "w_up": w_up, "w_down": w_down}


def reference(tokens, expert_ids, gate_values, w_gate, w_up, w_down):
    blocks = TOKENS // TOK_DEV
    pairs = expert_ids.reshape(blocks, TOK_DEV * TOP)
    onehot = (pairs[:, :, None] == jnp.arange(EXPERTS, dtype=jnp.int32)[None, None, :]).astype(jnp.int32)
    ranks = jnp.sum(jnp.cumsum(onehot, axis=1) * onehot, axis=2) - 1
    block_of = jnp.arange(blocks, dtype=jnp.int32)[:, None]
    flat_slot = pairs * (blocks * CAP) + block_of * CAP + ranks
    token_of = block_of * TOK_DEV + jnp.arange(TOK_DEV * TOP, dtype=jnp.int32)[None, :] // TOP
    table = jnp.zeros((EXPERTS * blocks * CAP,), jnp.int32).at[flat_slot.reshape(-1)].set(token_of.reshape(-1).astype(jnp.int32))
    weight_table = jnp.zeros((EXPERTS * blocks * CAP,), jnp.float32).at[flat_slot.reshape(-1)].set(gate_values.reshape(-1))
    width = FF // N_TENSOR

    def one_expert(total, inputs):
        index, weights, wg, wu, wd = inputs
        rows = tokens[index]
        gate = jnp.dot(rows, wg, preferred_element_type=jnp.float32)
        up = jnp.dot(rows, wu, preferred_element_type=jnp.float32)
        hidden = (jax.nn.silu(gate) * up).astype(jnp.bfloat16)
        summed = jnp.zeros((rows.shape[0], D), jnp.float32)
        for part in range(N_TENSOR):
            piece = jnp.dot(hidden[:, part * width:(part + 1) * width], wd[part * width:(part + 1) * width], preferred_element_type=jnp.float32)
            rounded = lax.optimization_barrier(piece.astype(jnp.bfloat16))
            summed = summed + rounded.astype(jnp.float32)
        out_rows = lax.optimization_barrier(summed.astype(jnp.bfloat16)).astype(jnp.float32)
        total = total.at[index].add(weights[:, None] * out_rows)
        return total, None

    start = jnp.zeros((TOKENS, D), jnp.float32)
    total, _ = lax.scan(one_expert, start, (table.reshape(EXPERTS, blocks * CAP), weight_table.reshape(EXPERTS, blocks * CAP), w_gate, w_up, w_down))
    return total.astype(jnp.bfloat16)
```

```python
import jax
import jax.numpy as jnp
from jax import lax
from jax.experimental import pallas as pl
from jax.experimental.pallas import tpu as pltpu
from jax.sharding import PartitionSpec as P

MESH = pl.DeviceIdType.MESH
BF = jnp.bfloat16
F32 = jnp.float32

NX, NY, NZ, NC = 4, 4, 8, 2
T = 16
S = 4
D = 7168
PLANE = NY * NZ * NC * T
SLOTS = NY * NZ * NC * S
W = 512
N = D // W
H = 256
DS = D // NX
W2 = 256
N2 = DS // W2


def here():
    e = lax.axis_index("expert")
    x = lax.axis_index("tensor")
    return e // (NZ * NC), (e // NC) % NZ, e % NC, x, e


def dev(y, z, c, x):
    return ((y * NZ + z) * NC + c, x)


def send(src, dst, ssem, rsem, device):
    pltpu.make_async_remote_copy(
        src_ref=src, dst_ref=dst, send_sem=ssem, recv_sem=rsem, device_id=device, device_id_type=MESH
    ).start()


def wait(ref, sem):
    pltpu.make_async_copy(ref, ref, sem).wait()


def greet(peers):
    barrier = pltpu.get_barrier_semaphore()
    for p in peers:
        pl.semaphore_signal(barrier, inc=1, device_id=p, device_id_type=MESH)
    pl.semaphore_wait(barrier, len(peers))


def iota(shape, axis):
    return lax.broadcasted_iota(jnp.int32, shape, axis)


def mm(a, b):
    return jnp.dot(a, b, preferred_element_type=F32)


def pick(meta, e):
    hot = (iota((8, 128), 1) == e).astype(BF)
    row = lax.dot_general(hot, meta, (((1,), (1,)), ((), ())), preferred_element_type=F32)[0:1]
    r = iota((SLOTS, PLANE), 0)
    t = iota((SLOTS, PLANE), 1)
    want = (r % S + 1).astype(F32)
    return jnp.where((t // T == r // S) & (row == want), 1.0, 0.0).astype(BF)


def dispatch_kernel(
    ids, gates, tok, wg, wu, wd, hid, meta_y, wdr,
    tokbuf, slotbuf, wbuf, acc, meta, sel,
    wsem, dsem, rsem_d, lsem, mz_s, mz_r, my_s, my_r, ms_s, ms_r, mx_s, mx_r, mq_s, mq_r,
    zs, zr, ys, yr, yfs, ss, sr, xs, xr, xfs,
):
    y, z, c, x, e = here()
    m8 = lambda v, k: pl.multiple_of(v, k)
    up_y, dn_y = (y + 1) % NY, (y + NY - 1) % NY
    up_x, dn_x = (x + 1) % NX, (x + NX - 1) % NX
    sib = dev(y, z, 1 - c, x)
    line = m8((c * NY + y) * NZ * T, 128)
    own = m8(((c * NY + y) * NZ + z) * T, 16)
    half = m8(c * (PLANE // 2), 512)

    @pl.loop(0, N)
    def _(j):
        pltpu.make_async_copy(wg.at[pl.ds(m8(j * W, W), W)], wbuf.at[j, :, 0:H], wsem.at[j]).start()
        pltpu.make_async_copy(wu.at[pl.ds(m8(j * W, W), W)], wbuf.at[j, :, H : 2 * H], wsem.at[j]).start()

    mine = wd.at[:, pl.ds(m8(x * DS, 256), DS)]
    keep = pltpu.make_async_copy(mine, wdr.at[pl.ds(m8(x * H, H), H)], lsem)
    keep.start()

    lane = iota((T, 128), 1) % 64
    hit = jnp.zeros((T, 128), F32)
    val = jnp.zeros((T, 128), F32)
    for k in range(8):
        eq = ids[:, k : k + 1] == lane
        hit = hit + jnp.where(eq, 1.0, 0.0)
        val = val + jnp.where(eq, gates[:, k : k + 1], 0.0)
    below = (iota((T, T), 1) < iota((T, T), 0)).astype(F32)
    rank = mm(below, hit)
    info = jnp.where(iota((T, 128), 1) < 64, hit * (rank + 1.0), val).astype(BF)
    mrow = m8(x * PLANE + own, 16)
    meta[pl.ds(mrow, T), :] = info
    for j in range(N):
        tokbuf[j, pl.ds(own, T), :] = tok[:, j * W : (j + 1) * W]

    greet(
        [dev(y, (z + d) % NZ, c, x) for d in range(1, NZ)]
        + [dev((y + d) % NY, z, c, x) for d in range(1, NY)]
        + [dev(y, z, c, (x + d) % NX) for d in range(1, NX)]
        + [sib]
    )

    far = (1, 7, 2, 6, 3, 5, 4)
    for d in far:
        send(meta.at[pl.ds(mrow, T)], meta.at[pl.ds(mrow, T)], mz_s, mz_r, dev(y, (z + d) % NZ, c, x))

    @pl.loop(0, N)
    def _(j):
        for d in far:
            send(
                tok.at[:, pl.ds(m8(j * W, W), W)], tokbuf.at[j, pl.ds(own, T)], zs, zr.at[j],
                dev(y, (z + d) % NZ, c, x),
            )

    wait(meta.at[0 : 7 * T], mz_r)
    mline = m8(x * PLANE + line, 128)
    for d in (1, 3, 2):
        send(meta.at[pl.ds(mline, 128)], meta.at[pl.ds(mline, 128)], my_s, my_r, dev((y + d) % NY, z, c, x))
    wait(meta.at[0 : 3 * 128], my_r)
    mhalf = m8(x * PLANE + half, 512)
    send(meta.at[pl.ds(mhalf, 512)], meta.at[pl.ds(mhalf, 512)], ms_s, ms_r, sib)
    for d in (1, 3, 2):
        send(meta.at[pl.ds(mhalf, 512)], meta.at[pl.ds(mhalf, 512)], mx_s, mx_r, dev(y, z, c, (x + d) % NX))

    def stage_y(j):
        wait(tokbuf.at[j, 0 : 7 * T], zr.at[j])
        rows = tokbuf.at[j, pl.ds(line, 128)]
        send(rows, rows, ys, yr.at[j, 0], dev(up_y, z, c, x))
        send(rows, rows, ys, yr.at[j, 1], dev(dn_y, z, c, x))

    def stage_yf(j):
        wait(tokbuf.at[j, 0:128], yr.at[j, 0])
        rows = tokbuf.at[j, pl.ds(m8((c * NY + dn_y) * 128, 128), 64)]
        send(rows, rows, yfs, yr.at[j, 2], dev(up_y, z, c, x))
        wait(tokbuf.at[j, 0:128], yr.at[j, 1])
        rows = tokbuf.at[j, pl.ds(m8((c * NY + up_y) * 128 + 64, 64), 64)]
        send(rows, rows, yfs, yr.at[j, 2], dev(dn_y, z, c, x))

    def stage_s(j):
        wait(tokbuf.at[j, 0:128], yr.at[j, 2])
        rows = tokbuf.at[j, pl.ds(half, 512)]
        send(rows, rows, ss, sr.at[j], sib)

    def stage_x(j):
        wait(tokbuf.at[j, 0:512], sr.at[j])
        slots = slotbuf.at[j, pl.ds(m8(x * SLOTS, SLOTS), SLOTS)]
        slots[...] = mm(sel[...], tokbuf[j]).astype(BF)
        send(slots, slots, xs, xr.at[j, 0], dev(y, z, c, up_x))
        send(slots, slots, xs, xr.at[j, 1], dev(y, z, c, dn_x))
        for d in (1, 3, 2):
            to = (x + d) % NX
            send(
                wd.at[:, pl.ds(m8(to * DS + j * 128, 128), 128)],
                wdr.at[pl.ds(m8(x * H, H), H), pl.ds(m8(j * 128, 128), 128)],
                dsem, rsem_d, dev(y, z, c, to),
            )

    def stage_xf(j):
        wait(slotbuf.at[j, 0:SLOTS], xr.at[j, 0])
        rows = slotbuf.at[j, pl.ds(m8(dn_x * SLOTS, SLOTS), SLOTS // 2)]
        send(rows, rows, xfs, xr.at[j, 2], dev(y, z, c, up_x))
        wait(slotbuf.at[j, 0:SLOTS], xr.at[j, 1])
        rows = slotbuf.at[j, pl.ds(m8(up_x * SLOTS + SLOTS // 2, SLOTS // 2), SLOTS // 2)]
        send(rows, rows, xfs, xr.at[j, 2], dev(y, z, c, dn_x))

    def stage_m(j):
        wait(slotbuf.at[j, 0:SLOTS], xr.at[j, 2])
        wait(wbuf.at[j], wsem.at[j])
        acc[...] += mm(slotbuf[j], wbuf[j])

    acc[...] = jnp.zeros_like(acc)
    stages = (stage_y, stage_yf, stage_s, stage_x, stage_xf, stage_m)

    def step(i, first, last):
        for k, stage in enumerate(stages):
            if first <= k <= last:

                @pl.when((i - k >= 0) & (i - k < N))
                def _(k=k, stage=stage):
                    stage(i - k)

    for i in range(3):
        for k in range(i + 1):
            stages[k](i - k)

    wait(meta.at[0:512], ms_r)
    plane = meta[pl.ds(m8(x * PLANE, PLANE), PLANE), :]
    sel[...] = pick(plane, e)

    @pl.loop(3, N + 5)
    def _(i):
        step(i, 0, 5)

    wait(meta.at[0 : 3 * 512], mx_r)
    for d in range(1, NX):
        rows = meta.at[pl.ds(m8((x + d) % NX * PLANE + half, 512), 512)]
        send(rows, rows, mq_s, mq_r, sib)
    wait(meta.at[0 : 3 * 512], mq_r)

    hot = (iota((128, 2 * 128), 0) == 64 + e).astype(BF)
    for q in range(NX):
        info = meta[q * PLANE : (q + 1) * PLANE, :]
        weight = mm(pick(info, e), mm(info, hot).astype(BF))
        part = acc[q * SLOTS : (q + 1) * SLOTS, :]
        gate, up = part[:, 0:H], part[:, H : 2 * H]
        hid[q * SLOTS : (q + 1) * SLOTS, :] = (gate / (1.0 + jnp.exp(-gate)) * up * weight).astype(BF)
        meta_y[q * 128 : (q + 1) * 128, :] = meta[pl.ds(m8(q * PLANE + line, 128), 128), :]

    keep.wait()
    wait(wdr.at[0 : 3 * H], rsem_d)
    wait(wdr.at[0 : 3 * H], dsem)
    wait(meta.at[0 : 7 * T], mz_s)
    wait(meta.at[0 : 3 * 128], my_s)
    wait(meta.at[0:512], ms_s)
    wait(meta.at[0 : 3 * 512], mx_s)
    wait(meta.at[0 : 3 * 512], mq_s)
    wait(tokbuf.at[:, 0 : 7 * T], zs)
    wait(tokbuf.at[:, 0:256], ys)
    wait(tokbuf.at[:, 0:128], yfs)
    wait(tokbuf.at[:, 0:512], ss)
    wait(slotbuf.at[:, 0 : 2 * SLOTS], xs)
    wait(slotbuf.at[:, 0:SLOTS], xfs)


def combine_kernel(
    hid, meta_y, wdr, out,
    hbuf, wbuf, obuf, ybuf, dbuf, zbuf, fbuf, place,
    wsem, hs, hfs, hr, ys, yr, zs, zr, xs, xr,
):
    y, z, c, x, e = here()
    m8 = lambda v, k: pl.multiple_of(v, k)
    up_x, dn_x = (x + 1) % NX, (x + NX - 1) % NX
    load = pltpu.make_async_copy(wdr, wbuf, wsem)
    load.start()
    hbuf[x] = hid[...]
    others = [dev((y + d) % NY, z, k, x) for d in range(1, NY) for k in range(NC)]
    greet(
        [dev(y, (z + d) % NZ, c, x) for d in range(1, NZ)]
        + [dev(y, z, c, (x + d) % NX) for d in range(1, NX)]
        + others
        + [dev(y, z, 1 - c, x)]
    )
    send(hbuf.at[x], hbuf.at[x], hs, hr.at[0], dev(y, z, c, up_x))
    send(hbuf.at[x], hbuf.at[x], hs, hr.at[1], dev(y, z, c, dn_x))

    rows, cols = NX * NZ * T, NC * NY * NX * NZ * S
    col = iota((128, cols), 1)
    source = col // (NX * NZ * S)
    expert = ((source % NY) * NZ + z) * NC + source // NY
    table = (iota((128, cols), 0) == expert).astype(BF)
    found = mm(meta_y[...], table)
    col = iota((rows, cols), 1)
    same = iota((rows, cols), 0) // T == (col // S) % (NX * NZ)
    place[...] = jnp.where(same & (found == (col % S + 1).astype(F32)), 1.0, 0.0).astype(BF)

    wait(hbuf.at[0], hr.at[0])
    send(hbuf.at[dn_x, 0:512], hbuf.at[dn_x, 0:512], hfs, hr.at[2], dev(y, z, c, up_x))
    wait(hbuf.at[0], hr.at[1])
    send(hbuf.at[up_x, 512:1024], hbuf.at[up_x, 512:1024], hfs, hr.at[2], dev(y, z, c, dn_x))
    load.wait()
    wait(hbuf.at[0], hr.at[2])

    def stage_y(j):
        at = pl.ds(m8(j * W2, W2), W2)
        total = mm(hbuf[0], wbuf[0:H, at])
        for q in range(1, NX):
            total = total + mm(hbuf[q], wbuf[q * H : (q + 1) * H, at])
        obuf[j] = total.astype(BF).reshape(NX, NC, NY, NZ * S, W2)
        ybuf[j, c * NY + y] = obuf[j, :, c, y]
        place_of = ybuf.at[j, c * NY + y]
        for d in (1, 3, 2):
            for k in range(NC):
                to = (y + d) % NY
                send(obuf.at[j, :, k, to], place_of, ys, yr.at[j], dev(to, z, k, x))
        send(obuf.at[j, :, 1 - c, y], place_of, ys, yr.at[j], dev(y, z, 1 - c, x))

    def stage_z(j):
        wait(ybuf.at[j, 0:7], yr.at[j])
        total = mm(place[...], ybuf[j].reshape(cols, W2))
        dbuf[j] = total.astype(BF).reshape(NX, NZ, T, W2)
        zbuf[j, z] = dbuf[j, :, z]
        for d in (1, 7, 2, 6, 3, 5, 4):
            to = (z + d) % NZ
            send(dbuf.at[j, :, to], zbuf.at[j, z], zs, zr.at[j], dev(y, to, c, x))

    def stage_x(j):
        wait(zbuf.at[j, 0:7], zr.at[j])
        fbuf[j] = jnp.sum(zbuf[j].astype(F32), axis=0).astype(BF)
        at = pl.ds(m8(x * DS + j * W2, W2), W2)
        out[:, at] = fbuf[j, x]
        for d in (1, 3, 2):
            to = (x + d) % NX
            send(fbuf.at[j, to], out.at[:, at], xs, xr, dev(y, z, c, to))

    stages = (stage_y, stage_z, stage_x)

    @pl.loop(0, N2 + 2)
    def _(i):
        for k, stage in enumerate(stages):

            @pl.when((i - k >= 0) & (i - k < N2))
            def _(k=k, stage=stage):
                stage(i - k)

    wait(out.at[:, 0 : 3 * DS], xr)
    wait(out.at[:, 0 : 3 * DS], xs)
    wait(hbuf.at[0:2], hs)
    wait(hbuf.at[0], hfs)
    wait(ybuf.at[:, 0:7], ys)
    wait(zbuf.at[:, 0:7], zs)


def local(tokens, expert_ids, gate_values, w_gate, w_up, w_down):
    vm = pl.BlockSpec(memory_space=pltpu.VMEM)
    hb = pl.BlockSpec(memory_space=pl.ANY)
    dma = pltpu.SemaphoreType.DMA
    hid, meta_y, wdr = pl.pallas_call(
        dispatch_kernel,
        out_shape=(
            jax.ShapeDtypeStruct((NX * SLOTS, H), BF),
            jax.ShapeDtypeStruct((NX * NZ * T, 128), BF),
            jax.ShapeDtypeStruct((NX * H, DS), BF),
        ),
        in_specs=[vm, vm, vm, hb, hb, hb],
        out_specs=(vm, vm, hb),
        scratch_shapes=[
            pltpu.VMEM((N, PLANE, W), BF),
            pltpu.VMEM((N, NX * SLOTS, W), BF),
            pltpu.VMEM((N, W, 2 * H), BF),
            pltpu.VMEM((NX * SLOTS, 2 * H), F32),
            pltpu.VMEM((NX * PLANE, 128), BF),
            pltpu.VMEM((SLOTS, PLANE), BF),
            dma((N,)), dma, dma, dma,
            dma, dma, dma, dma, dma, dma, dma, dma, dma, dma,
            dma, dma((N,)), dma, dma((N, 3)), dma, dma, dma((N,)), dma, dma((N, 3)), dma,
        ],
        compiler_params=pltpu.CompilerParams(
            collective_id=0, has_side_effects=True, vmem_limit_bytes=58 << 20
        ),
        name="dispatch",
    )(expert_ids, gate_values, tokens, w_gate[0], w_up[0], w_down[0])
    return pl.pallas_call(
        combine_kernel,
        out_shape=jax.ShapeDtypeStruct((T, D), BF),
        in_specs=[vm, vm, hb],
        out_specs=vm,
        scratch_shapes=[
            pltpu.VMEM((NX, NX * SLOTS, H), BF),
            pltpu.VMEM((NX * H, DS), BF),
            pltpu.VMEM((N2, NX, NC, NY, NZ * S, W2), BF),
            pltpu.VMEM((N2, NC * NY, NX, NZ * S, W2), BF),
            pltpu.VMEM((N2, NX, NZ, T, W2), BF),
            pltpu.VMEM((N2, NZ, NX, T, W2), BF),
            pltpu.VMEM((N2, NX, T, W2), BF),
            pltpu.VMEM((NX * NZ * T, NC * NY * NX * NZ * S), BF),
            dma, dma, dma, dma((3,)), dma, dma((N2,)), dma, dma((N2,)), dma, dma,
        ],
        compiler_params=pltpu.CompilerParams(
            collective_id=1, has_side_effects=True, vmem_limit_bytes=48 << 20
        ),
        name="combine",
    )(hid, meta_y, wdr)


def solution(mesh):
    return jax.shard_map(
        local,
        mesh=mesh,
        in_specs=(
            P(("expert", "tensor"), None),
            P(("expert", "tensor"), None),
            P(("expert", "tensor"), None),
            P("expert", None, "tensor"),
            P("expert", None, "tensor"),
            P("expert", "tensor", None),
        ),
        out_specs=P(("expert", "tensor"), None),
        check_vma=False,
    )
```

```python
import jax
import jax.numpy as jnp
from jax import lax
from jax.experimental import pallas as pl
from jax.experimental.pallas import tpu as pltpu
from jax.sharding import PartitionSpec as P

MESH = pl.DeviceIdType.MESH
BF = jnp.bfloat16
F32 = jnp.float32

NX, NY, NZ, NC = 4, 4, 8, 2
T = 16
S = 4
D = 7168
PLANE = NY * NZ * NC * T
SLOTS = NY * NZ * NC * S
WA, WB, WC = 512, 256, 128
G = WA + WB + WC
N = D // G
H = 256
DS = D // NX
W2 = 256
N2 = DS // W2


def here():
    e = lax.axis_index("expert")
    x = lax.axis_index("tensor")
    return e // (NZ * NC), (e // NC) % NZ, e % NC, x, e


def dev(y, z, c, x):
    return ((y * NZ + z) * NC + c, x)


def send(src, dst, ssem, rsem, device):
    pltpu.make_async_remote_copy(
        src_ref=src, dst_ref=dst, send_sem=ssem, recv_sem=rsem, device_id=device, device_id_type=MESH
    ).start()


def wait(ref, sem):
    pltpu.make_async_copy(ref, ref, sem).wait()


def iota(shape, axis):
    return lax.broadcasted_iota(jnp.int32, shape, axis)


def mm(a, b):
    return jnp.dot(a, b, preferred_element_type=F32)


def pick(meta, e):
    hot = (iota((8, 128), 1) == e).astype(BF)
    row = lax.dot_general(hot, meta, (((1,), (1,)), ((), ())), preferred_element_type=F32)[0:1]
    r = iota((SLOTS, PLANE), 0)
    t = iota((SLOTS, PLANE), 1)
    want = (r % S + 1).astype(F32)
    return jnp.where((t // T == r // S) & (row == want), 1.0, 0.0).astype(BF)


def layer_kernel(
    ids, gates, tok, wg, wu, wd, out,
    abuf, slotbuf, bbuf, cbuf, wbuf, acc, meta, sel, wdv, hbuf, ybuf, zbuf, fbuf, place,
    wsem, ds, dr, keep_sem, tsem, ms, mr,
    az_s, az_r, ay_s, ay_r, ayf_s, as_s, as_r, ax_s, ax_r, axf_s,
    bx_s, bx_r, bz_s, bz_r, by_s, by_r, byf_s, bs_s, bs_r,
    cx_s, cx_r, cy_s, cy_r, cz_s, cz_r, cs_s, cs_r,
    h_s, h_r, oy_s, oy_r, oz_s, oz_r, ox_s, ox_r,
):
    y, z, c, x, e = here()
    m8 = pl.multiple_of
    up_y, dn_y = dev((y + 1) % NY, z, c, x), dev((y + NY - 1) % NY, z, c, x)
    up_z, dn_z = dev(y, (z + 1) % NZ, c, x), dev(y, (z + NZ - 1) % NZ, c, x)
    up_x, dn_x = dev(y, z, c, (x + 1) % NX), dev(y, z, c, (x + NX - 1) % NX)
    sib = dev(y, z, 1 - c, x)
    zd = (1, 7, 2, 6, 3, 5, 4)
    xs = [dev(y, z, c, (x + d) % NX) for d in (1, 3, 2)]
    ys = [dev((y + d) % NY, z, c, x) for d in (1, 3, 2)]
    zs = [dev(y, (z + d) % NZ, c, x) for d in zd]
    yat = lambda d: (y + NY + d) % NY
    zat = lambda d: (z + NZ + d) % NZ
    xat = lambda d: (x + NX + d) % NX

    barrier = pltpu.get_barrier_semaphore()
    peers = zs + ys + xs + [sib] + [dev(yat(d), z, 1 - c, x) for d in (1, 3, 2)]
    for p in peers:
        pl.semaphore_signal(barrier, inc=1, device_id=p, device_id_type=MESH)

    for j in range(N):
        at = j * G
        pltpu.make_async_copy(tok.at[:, at : at + WA], abuf.at[j, c, y, z], tsem).start()
        pltpu.make_async_copy(tok.at[:, at + WA : at + WA + WB], bbuf.at[j, x, c, y, z], tsem).start()
        pltpu.make_async_copy(tok.at[:, at + WA + WB : at + G], cbuf.at[j, x, c, y, z], tsem).start()
    mine = pl.ds(m8(x * H, H), H)
    keep = pltpu.make_async_copy(wd.at[:, pl.ds(m8(x * DS, 256), DS)], wdv.at[mine], keep_sem)
    keep.start()

    lane = iota((128, T), 0) % 64
    hit = jnp.zeros((128, T), F32)
    val = jnp.zeros((128, T), F32)
    for k in range(8):
        eq = ids[k : k + 1, :] == lane
        hit = hit + jnp.where(eq, 1.0, 0.0)
        val = val + jnp.where(eq, gates[k : k + 1, :], 0.0)
    before = (iota((T, T), 0) < iota((T, T), 1)).astype(F32)
    rank = mm(hit, before)
    info = jnp.where(iota((128, T), 0) < 64, hit * (rank + 1.0), val).astype(BF)
    eye = (iota((T, T), 0) == iota((T, T), 1)).astype(BF)
    meta[x, c, y, z] = lax.dot_general(
        eye, info, (((1,), (1,)), ((), ())), preferred_element_type=F32
    ).astype(BF)
    acc[...] = jnp.zeros_like(acc)
    wait(tok, tsem)

    pl.semaphore_wait(barrier, len(peers))

    def a_z(j):
        for p in zs:
            send(abuf.at[j, c, y, z], abuf.at[j, c, y, z], az_s, az_r.at[j], p)

    a_z(0)
    for p in zs:
        send(meta.at[x, c, y, z], meta.at[x, c, y, z], ms.at[0], mr.at[0], p)
    for p in xs:
        send(bbuf.at[:, x, c, y, z], bbuf.at[:, x, c, y, z], bx_s, bx_r, p)
    for p in xs:
        send(cbuf.at[:, x, c, y, z], cbuf.at[:, x, c, y, z], cx_s, cx_r, p)
    a_z(1)

    def routing():
        wait(meta.at[0, 0, 0, 0:7], mr.at[0])
        for p in ys:
            send(meta.at[x, c, y], meta.at[x, c, y], ms.at[1], mr.at[1], p)

    def routing_half():
        wait(meta.at[0, 0, 0:3], mr.at[1])
        send(meta.at[x, c], meta.at[x, c], ms.at[2], mr.at[2], sib)
        for p in xs:
            send(meta.at[x, c], meta.at[x, c], ms.at[3], mr.at[3], p)

    def routing_plane():
        wait(meta.at[0, 0], mr.at[2])
        sel[x] = pick(meta[x].reshape(PLANE, 128), e)
        wait(meta.at[0:3, 0], mr.at[3])
        for d in (1, 2, 3):
            send(meta.at[xat(d), c], meta.at[xat(d), c], ms.at[4], mr.at[4], sib)

    def routing_rest():
        wait(meta.at[0:3, 0], mr.at[4])
        for d in (1, 2, 3):
            sel[xat(d)] = pick(meta[xat(d)].reshape(PLANE, 128), e)

    def a_y(j):
        wait(abuf.at[j, 0, 0, 0:7], az_r.at[j])
        rows = abuf.at[j, c, y]
        send(rows, rows, ay_s, ay_r.at[j, 0], up_y)
        send(rows, rows, ay_s, ay_r.at[j, 1], dn_y)

    def a_yf(j):
        wait(abuf.at[j, 0, 0], ay_r.at[j, 0])
        rows = abuf.at[j, c, yat(-1), 0:4]
        send(rows, rows, ayf_s, ay_r.at[j, 2], up_y)
        wait(abuf.at[j, 0, 0], ay_r.at[j, 1])
        rows = abuf.at[j, c, yat(1), 4:8]
        send(rows, rows, ayf_s, ay_r.at[j, 2], dn_y)

    def a_s(j):
        wait(abuf.at[j, 0, 0], ay_r.at[j, 2])
        send(abuf.at[j, c], abuf.at[j, c], as_s, as_r.at[j], sib)

    def a_x(j):
        wait(abuf.at[j, 0], as_r.at[j])
        slotbuf[j, x] = mm(sel[x], abuf[j].reshape(PLANE, WA)).astype(BF)
        slots = slotbuf.at[j, x]
        send(slots, slots, ax_s, ax_r.at[j, 0], up_x)
        send(slots, slots, ax_s, ax_r.at[j, 1], dn_x)

    def a_xf(j):
        wait(slotbuf.at[j, 0], ax_r.at[j, 0])
        rows = slotbuf.at[j, xat(-1), 0 : SLOTS // 2]
        send(rows, rows, axf_s, ax_r.at[j, 2], up_x)
        wait(slotbuf.at[j, 0], ax_r.at[j, 1])
        rows = slotbuf.at[j, xat(1), SLOTS // 2 : SLOTS]
        send(rows, rows, axf_s, ax_r.at[j, 2], dn_x)

    def b_z(j):
        @pl.when(j == 0)
        def _():
            wait(bbuf.at[:, 0, 0, 0, 0:3], bx_r)

        rows = bbuf.at[j, :, c, y, z]
        for p in zs:
            send(rows, rows, bz_s, bz_r.at[j], p)

    def b_y(j):
        wait(bbuf.at[j, :, 0, 0, 0:7], bz_r.at[j])
        rows = bbuf.at[j, :, c, y]
        send(rows, rows, by_s, by_r.at[j, 0], up_y)
        send(rows, rows, by_s, by_r.at[j, 1], dn_y)

    def b_yf(j):
        wait(bbuf.at[j, :, 0, 0], by_r.at[j, 0])
        rows = bbuf.at[j, 0:2, c, yat(-1)]
        send(rows, rows, byf_s, by_r.at[j, 2], up_y)
        wait(bbuf.at[j, :, 0, 0], by_r.at[j, 1])
        rows = bbuf.at[j, 2:4, c, yat(1)]
        send(rows, rows, byf_s, by_r.at[j, 2], dn_y)

    def b_s(j):
        wait(bbuf.at[j, :, 0, 0], by_r.at[j, 2])
        send(bbuf.at[j, :, c], bbuf.at[j, :, c], bs_s, bs_r.at[j], sib)

    def c_y(j):
        @pl.when(j == 0)
        def _():
            wait(cbuf.at[:, 0, 0, 0, 0:3], cx_r)

        rows = cbuf.at[j, :, c, y, z]
        for p in ys:
            send(rows, rows, cy_s, cy_r.at[j], p)

    def c_z(j):
        wait(cbuf.at[j, :, 0, 0, 0:3], cy_r.at[j])
        rows = cbuf.at[j, :, c, :, z]
        send(rows, rows, cz_s, cz_r.at[j, 0], up_z)
        send(rows, rows, cz_s, cz_r.at[j, 1], dn_z)

    def c_hop(j, k):
        block = cbuf.at[j, :, 0, :, 0]
        wait(block, cz_r.at[j, 2 * k - 2])
        rows = cbuf.at[j, :, c, :, zat(-k)]
        send(rows, rows, cz_s, cz_r.at[j, 2 * k], up_z)
        wait(block, cz_r.at[j, 2 * k - 1])
        rows = cbuf.at[j, :, c, :, zat(k)]
        send(rows, rows, cz_s, cz_r.at[j, 2 * k + 1], dn_z)

    def c_last(j):
        block = cbuf.at[j, :, 0, :, 0]
        wait(block, cz_r.at[j, 4])
        rows = cbuf.at[j, 0:2, c, :, zat(-3)]
        send(rows, rows, cz_s, cz_r.at[j, 6], up_z)
        wait(block, cz_r.at[j, 5])
        rows = cbuf.at[j, 2:4, c, :, zat(3)]
        send(rows, rows, cz_s, cz_r.at[j, 6], dn_z)

    def c_s(j):
        wait(cbuf.at[j, :, 0, :, 0], cz_r.at[j, 6])
        send(cbuf.at[j, :, c], cbuf.at[j, :, c], cs_s, cs_r.at[j], sib)

    def w_d(j):
        rows = pl.ds(m8(j * (H // 8), 32), H // 8)
        there = pl.ds(m8(x * H + j * (H // 8), 32), H // 8)
        for d, p in zip((1, 3, 2), xs):
            send(wd.at[rows, pl.ds(m8(xat(d) * DS, 256), DS)], wdv.at[there], ds, dr, p)

    def load(j):
        rows = pl.ds(m8(j * G, 128), G)
        pltpu.make_async_copy(wg.at[rows], wbuf.at[j % 3, :, 0:H], wsem.at[j % 3]).start()
        pltpu.make_async_copy(wu.at[rows], wbuf.at[j % 3, :, H : 2 * H], wsem.at[j % 3]).start()

    def multiply(j):
        wait(slotbuf.at[j, 0], ax_r.at[j, 2])
        wait(bbuf.at[j, :, 0], bs_r.at[j])
        wait(cbuf.at[j, :, 0], cs_r.at[j])
        k = j % 3
        wait(wbuf.at[k], wsem.at[k])
        for q in range(NX):
            total = mm(slotbuf[j, q], wbuf[k, 0:WA])
            rows = mm(sel[q], bbuf[j, q].reshape(PLANE, WB)).astype(BF)
            total = total + mm(rows, wbuf[k, WA : WA + WB])
            rows = mm(sel[q], cbuf[j, q].reshape(PLANE, WC)).astype(BF)
            acc[q] += total + mm(rows, wbuf[k, WA + WB : G])

    stages = (
        (-2, a_z), (0, b_z), (0, c_y), (0, a_y),
        (1, a_yf), (1, b_y), (1, c_z),
        (2, a_s), (2, b_yf), (2, lambda j: c_hop(j, 1)),
        (3, a_x), (3, b_s), (3, lambda j: c_hop(j, 2)),
        (4, a_xf), (4, c_last), (4, load), (5, c_s), (6, multiply),
    )

    @pl.loop(0, N + 6)
    def _(i):
        @pl.when(i < 4)
        def _():
            w_d(2 * i)
            w_d(2 * i + 1)

        pl.when(i == 0)(routing)
        pl.when(i == 1)(routing_half)
        pl.when(i == 3)(routing_plane)
        pl.when(i == 5)(routing_rest)
        for k, stage in stages:

            @pl.when((i - k >= max(0, -k)) & (i - k < N))
            def _(k=k, stage=stage):
                stage(i - k)

    hot = (iota((128, 2 * 128), 0) == 64 + e).astype(BF)
    for q in range(NX):
        weight = mm(sel[q], mm(meta[q].reshape(PLANE, 128), hot).astype(BF))
        gate, up = acc[q, :, 0:H], acc[q, :, H : 2 * H]
        hbuf[x, q] = (gate / (1.0 + jnp.exp(-gate)) * up * weight).astype(BF)
        for p in xs:
            send(hbuf.at[x, q], hbuf.at[x, q], h_s, h_r.at[q], p)

    cols = NC * NY * NZ * S
    col = iota((128, cols), 1)
    source = col // (NZ * S)
    expert = ((source % NY) * NZ + z) * NC + source // NY
    table = (iota((128, cols), 0) == expert).astype(BF)
    same = iota((NZ * T, cols), 0) // T == (col // S) % NZ
    for q in range(NX):
        found = mm(meta[q, c, y].reshape(NZ * T, 128), table)
        place[q] = jnp.where(same & (found == (col % S + 1).astype(F32)), 1.0, 0.0).astype(BF)

    wait(abuf.at[:, 0, 0, 0:7], az_s)
    wait(abuf.at[:, 0, 0:2], ay_s)
    wait(abuf.at[:, 0, 0:1], ayf_s)
    wait(abuf.at[:, 0], as_s)
    wait(bbuf.at[:, 0, 0, 0, 0:3], bx_s)
    wait(bbuf.at[:, :, 0, 0, 0:7], bz_s)
    wait(bbuf.at[:, 0], by_s)
    wait(bbuf.at[:, 0, 0], byf_s)
    wait(bbuf.at[:, 0:2], bs_s)
    keep.wait()
    wait(wdv.at[0 : 3 * H], dr)

    parts = ((0, 4), (4, 3))

    def o_y(q, h):
        p0, n = parts[h]
        if h == 0:
            wait(hbuf.at[0:3, 0], h_r.at[q])
        total = mm(hbuf[0, q], wdv[0:H, p0 * W2 : (p0 + n) * W2])
        for t in range(1, NX):
            total = total + mm(hbuf[t, q], wdv[t * H : (t + 1) * H, p0 * W2 : (p0 + n) * W2])
        total = total.astype(BF)
        for p in range(n):
            bbuf[p0 + p, q, :, :, 0:2] = total[:, p * W2 : (p + 1) * W2].reshape(NC, NY, 2, T, W2)
            ybuf[q, p0 + p, c * NY + y] = bbuf[p0 + p, q, c, y, 0:2]
        there = ybuf.at[q, p0 : p0 + n, c * NY + y]
        for d in (1, 3, 2):
            for k in (c, 1 - c):
                to = yat(d)
                send(bbuf.at[p0 : p0 + n, q, k, to, 0:2], there, oy_s, oy_r.at[q, h], dev(to, z, k, x))
        send(bbuf.at[p0 : p0 + n, q, 1 - c, y, 0:2], there, oy_s, oy_r.at[q, h], sib)

    def o_z(q, h):
        p0, n = parts[h]
        wait(ybuf.at[q, p0 : p0 + n, 0:7], oy_r.at[q, h])
        for p in range(p0, p0 + n):
            total = mm(place[q], ybuf[q, p].reshape(cols, W2)).astype(BF).reshape(NZ, T, W2)
            abuf[p, 0, q, :, :, 0:W2] = total
            zbuf[q, p, z] = abuf[p, 0, q, z, :, 0:W2]
        for d, dst in zip(zd, zs):
            send(
                abuf.at[p0 : p0 + n, 0, q, zat(d), :, 0:W2], zbuf.at[q, p0 : p0 + n, z],
                oz_s, oz_r.at[q, h], dst,
            )

    def o_x(q, h):
        p0, n = parts[h]
        wait(zbuf.at[q, p0 : p0 + n, 0:7], oz_r.at[q, h])
        for p in range(p0, p0 + n):
            fbuf[q, :, p * W2 : (p + 1) * W2] = jnp.sum(zbuf[q, p].astype(F32), axis=0).astype(BF)
        at = pl.ds(m8(x * DS + p0 * W2, W2), n * W2)
        here_part = fbuf.at[q, :, p0 * W2 : (p0 + n) * W2]

        @pl.when(q == x)
        def _():
            out[:, at] = here_part[...]

        @pl.when(q != x)
        def _():
            send(here_part, out.at[:, at], ox_s, ox_r, dev(y, z, c, q))

    @pl.loop(0, NX + 1)
    def _(q):
        for last, d, h, stage in (
            (0, 0, 0, o_y), (1, 1, 1, o_z), (1, 1, 0, o_x),
            (0, 0, 1, o_y), (0, 0, 0, o_z), (1, 1, 1, o_x),
        ):

            @pl.when((q - d >= 0) & (q - d < NX))
            def _(d=d, h=h, stage=stage):
                stage(q - d, h)

    wait(out.at[:, 0 : 3 * DS], ox_r)
    wait(out.at[:, 0 : 3 * DS], ox_s)
    wait(hbuf.at[0:3], h_s)
    wait(ybuf.at[:, :, 0:7], oy_s)
    wait(zbuf.at[:, :, 0:7], oz_s)
    wait(wdv.at[0 : 3 * H], ds)
    wait(meta.at[0, 0, 0, 0:7], ms.at[0])
    wait(meta.at[0, 0, 0:3], ms.at[1])
    wait(meta.at[0, 0], ms.at[2])
    wait(meta.at[0:3, 0], ms.at[3])
    wait(meta.at[0:3, 0], ms.at[4])
    wait(slotbuf.at[:, 0:2], ax_s)
    wait(slotbuf.at[:, 0:1], axf_s)
    wait(cbuf.at[:, 0, 0, 0, 0:3], cx_s)
    wait(cbuf.at[:, :, 0, 0, 0:3], cy_s)
    wait(cbuf.at[:, :, 0, :, 0:7], cz_s)
    wait(cbuf.at[:, 0:2], cs_s)


def local(tokens, expert_ids, gate_values, w_gate, w_up, w_down):
    vm = pl.BlockSpec(memory_space=pltpu.VMEM)
    hb = pl.BlockSpec(memory_space=pl.ANY)
    dma = pltpu.SemaphoreType.DMA
    return pl.pallas_call(
        layer_kernel,
        out_shape=jax.ShapeDtypeStruct((T, D), BF),
        in_specs=[vm, vm, hb, hb, hb, hb],
        out_specs=vm,
        scratch_shapes=[
            pltpu.VMEM((N, NC, NY, NZ, T, WA), BF),
            pltpu.VMEM((N, NX, SLOTS, WA), BF),
            pltpu.VMEM((N, NX, NC, NY, NZ, T, WB), BF),
            pltpu.VMEM((N, NX, NC, NY, NZ, T, WC), BF),
            pltpu.VMEM((3, G, 2 * H), BF),
            pltpu.VMEM((NX, SLOTS, 2 * H), F32),
            pltpu.VMEM((NX, NC, NY, NZ, T, 128), BF),
            pltpu.VMEM((NX, SLOTS, PLANE), BF),
            pltpu.VMEM((NX * H, DS), BF),
            pltpu.VMEM((NX, NX, SLOTS, H), BF),
            pltpu.VMEM((NX, N2, NC * NY, 2, T, W2), BF),
            pltpu.VMEM((NX, N2, NZ, T, W2), BF),
            pltpu.VMEM((NX, T, DS), BF),
            pltpu.VMEM((NX, NZ * T, NC * NY * NZ * S), BF),
            dma((3,)), dma, dma, dma, dma, dma((5,)), dma((5,)),
            dma, dma((N,)), dma, dma((N, 3)), dma, dma, dma((N,)), dma, dma((N, 3)), dma,
            dma, dma, dma, dma((N,)), dma, dma((N, 3)), dma, dma, dma((N,)),
            dma, dma, dma, dma((N,)), dma, dma((N, 7)), dma, dma((N,)),
            dma, dma((NX,)), dma, dma((NX, 2)), dma, dma((NX, 2)), dma, dma,
        ],
        compiler_params=pltpu.CompilerParams(
            collective_id=0, has_side_effects=True, vmem_limit_bytes=63 << 20
        ),
        name="layer",
    )(expert_ids.T, gate_values.T, tokens, w_gate[0], w_up[0], w_down[0])


def solution(mesh):
    return jax.shard_map(
        local,
        mesh=mesh,
        in_specs=(
            P(("expert", "tensor"), None),
            P(("expert", "tensor"), None),
            P(("expert", "tensor"), None),
            P("expert", None, "tensor"),
            P("expert", None, "tensor"),
            P("expert", "tensor", None),
        ),
        out_specs=P(("expert", "tensor"), None),
        check_vma=False,
    )
```

```python
import jax
import jax.numpy as jnp
from jax import lax
from jax.experimental import pallas as pl
from jax.experimental.pallas import tpu as pltpu
from jax.sharding import PartitionSpec as P

MESH = pl.DeviceIdType.MESH
BF = jnp.bfloat16
F32 = jnp.float32

NX, NY, NZ, NC = 4, 4, 8, 2
T = 16
S = 4
D = 7168
PLANE = NY * NZ * NC * T
SLOTS = NY * NZ * NC * S
WA, WB, WC = 512, 256, 128
G = WA + WB + WC
N = D // G
H = 256
DS = D // NX
W2 = 256
N2 = DS // W2


def here():
    e = lax.axis_index("expert")
    x = lax.axis_index("tensor")
    return e // (NZ * NC), (e // NC) % NZ, e % NC, x, e


def dev(y, z, c, x):
    return ((y * NZ + z) * NC + c, x)


def send(src, dst, ssem, rsem, device):
    pltpu.make_async_remote_copy(
        src_ref=src, dst_ref=dst, send_sem=ssem, recv_sem=rsem, device_id=device, device_id_type=MESH
    ).start()


def wait(ref, sem):
    pltpu.make_async_copy(ref, ref, sem).wait()


def iota(shape, axis):
    return lax.broadcasted_iota(jnp.int32, shape, axis)


def mm(a, b):
    return jnp.dot(a, b, preferred_element_type=F32)


def pick(meta, e):
    hot = (iota((8, 128), 1) == e).astype(BF)
    row = lax.dot_general(hot, meta, (((1,), (1,)), ((), ())), preferred_element_type=F32)[0:1]
    r = iota((SLOTS, PLANE), 0)
    t = iota((SLOTS, PLANE), 1)
    want = (r % S + 1).astype(F32)
    return jnp.where((t // T == r // S) & (row == want), 1.0, 0.0).astype(BF)


def layer_kernel(
    ids, gates, tok, wg, wu, wd, out,
    abuf, slotbuf, bbuf, cbuf, wbuf, acc, meta, sel, wdv, hbuf, ybuf, zbuf, fbuf, place,
    wsem, ds, dr, keep_sem, tsem, ms, mr,
    az_s, az_r, ay_s, ay_r, ayf_s, as_s, as_r, ax_s, ax_r, axf_s,
    bx_s, bx_r, bz_s, bz_r, by_s, by_r, byf_s, bs_s, bs_r,
    cx_s, cx_r, cy_s, cy_r, cz_s, cz_r, cs_s, cs_r,
    h_s, h_r, oy_s, oy_r, oz_s, oz_r, ox_s, ox_r,
):
    y, z, c, x, e = here()
    m8 = pl.multiple_of
    up_y, dn_y = dev((y + 1) % NY, z, c, x), dev((y + NY - 1) % NY, z, c, x)
    up_z, dn_z = dev(y, (z + 1) % NZ, c, x), dev(y, (z + NZ - 1) % NZ, c, x)
    up_x, dn_x = dev(y, z, c, (x + 1) % NX), dev(y, z, c, (x + NX - 1) % NX)
    sib = dev(y, z, 1 - c, x)
    zd = (1, 7, 2, 6, 3, 5, 4)
    xs = [dev(y, z, c, (x + d) % NX) for d in (1, 3, 2)]
    ys = [dev((y + d) % NY, z, c, x) for d in (1, 3, 2)]
    zs = [dev(y, (z + d) % NZ, c, x) for d in zd]
    yat = lambda d: (y + NY + d) % NY
    zat = lambda d: (z + NZ + d) % NZ
    xat = lambda d: (x + NX + d) % NX

    barrier = pltpu.get_barrier_semaphore()
    peers = zs + ys + xs + [sib] + [dev(yat(d), z, 1 - c, x) for d in (1, 3, 2)]
    for p in peers:
        pl.semaphore_signal(barrier, inc=1, device_id=p, device_id_type=MESH)

    for j in range(N):
        at = j * G
        pltpu.make_async_copy(tok.at[:, at : at + WA], abuf.at[j, c, y, z], tsem).start()
        pltpu.make_async_copy(tok.at[:, at + WA : at + WA + WB], bbuf.at[j, x, c, y, z], tsem).start()
        pltpu.make_async_copy(tok.at[:, at + WA + WB : at + G], cbuf.at[j, x, c, y, z], tsem).start()
    mine = pl.ds(m8(x * H, H), H)
    keep = pltpu.make_async_copy(wd.at[:, pl.ds(m8(x * DS, 256), DS)], wdv.at[mine], keep_sem)
    keep.start()

    lane = iota((128, T), 0) % 64
    hit = jnp.zeros((128, T), F32)
    val = jnp.zeros((128, T), F32)
    for k in range(8):
        eq = ids[k : k + 1, :] == lane
        hit = hit + jnp.where(eq, 1.0, 0.0)
        val = val + jnp.where(eq, gates[k : k + 1, :], 0.0)
    before = (iota((T, T), 0) < iota((T, T), 1)).astype(F32)
    rank = mm(hit, before)
    info = jnp.where(iota((128, T), 0) < 64, hit * (rank + 1.0), val).astype(BF)
    eye = (iota((T, T), 0) == iota((T, T), 1)).astype(BF)
    meta[x, c, y, z] = lax.dot_general(
        eye, info, (((1,), (1,)), ((), ())), preferred_element_type=F32
    ).astype(BF)
    acc[...] = jnp.zeros_like(acc)
    wait(tok, tsem)

    pl.semaphore_wait(barrier, len(peers))

    def a_z(j):
        for p in zs:
            send(abuf.at[j, c, y, z], abuf.at[j, c, y, z], az_s, az_r.at[j], p)

    a_z(0)
    for p in zs:
        send(meta.at[x, c, y, z], meta.at[x, c, y, z], ms.at[0], mr.at[0], p)
    for p in xs:
        send(bbuf.at[:, x, c, y, z], bbuf.at[:, x, c, y, z], bx_s, bx_r, p)
    for p in xs:
        send(cbuf.at[:, x, c, y, z], cbuf.at[:, x, c, y, z], cx_s, cx_r, p)
    a_z(1)

    def routing():
        wait(meta.at[0, 0, 0, 0:7], mr.at[0])
        for p in ys:
            send(meta.at[x, c, y], meta.at[x, c, y], ms.at[1], mr.at[1], p)

    def routing_half():
        wait(meta.at[0, 0, 0:3], mr.at[1])
        send(meta.at[x, c], meta.at[x, c], ms.at[2], mr.at[2], sib)
        for p in xs:
            send(meta.at[x, c], meta.at[x, c], ms.at[3], mr.at[3], p)

    def routing_plane():
        wait(meta.at[0, 0], mr.at[2])
        sel[x] = pick(meta[x].reshape(PLANE, 128), e)
        wait(meta.at[0:3, 0], mr.at[3])
        for d in (1, 2, 3):
            send(meta.at[xat(d), c], meta.at[xat(d), c], ms.at[4], mr.at[4], sib)

    def routing_rest():
        wait(meta.at[0:3, 0], mr.at[4])
        for d in (1, 2, 3):
            sel[xat(d)] = pick(meta[xat(d)].reshape(PLANE, 128), e)

    def a_y(j):
        wait(abuf.at[j, 0, 0, 0:7], az_r.at[j])
        rows = abuf.at[j, c, y]
        send(rows, rows, ay_s, ay_r.at[j, 0], up_y)
        send(rows, rows, ay_s, ay_r.at[j, 1], dn_y)

    def a_yf(j):
        wait(abuf.at[j, 0, 0], ay_r.at[j, 0])
        rows = abuf.at[j, c, yat(-1), 0:4]
        send(rows, rows, ayf_s, ay_r.at[j, 2], up_y)
        wait(abuf.at[j, 0, 0], ay_r.at[j, 1])
        rows = abuf.at[j, c, yat(1), 4:8]
        send(rows, rows, ayf_s, ay_r.at[j, 2], dn_y)

    def a_s(j):
        wait(abuf.at[j, 0, 0], ay_r.at[j, 2])
        send(abuf.at[j, c], abuf.at[j, c], as_s, as_r.at[j], sib)

    def a_x(j):
        wait(abuf.at[j, 0], as_r.at[j])
        slotbuf[j, x] = mm(sel[x], abuf[j].reshape(PLANE, WA)).astype(BF)
        slots = slotbuf.at[j, x]
        send(slots, slots, ax_s, ax_r.at[j, 0], up_x)
        send(slots, slots, ax_s, ax_r.at[j, 1], dn_x)

    def a_xf(j):
        wait(slotbuf.at[j, 0], ax_r.at[j, 0])
        rows = slotbuf.at[j, xat(-1), 0 : SLOTS // 2]
        send(rows, rows, axf_s, ax_r.at[j, 2], up_x)
        wait(slotbuf.at[j, 0], ax_r.at[j, 1])
        rows = slotbuf.at[j, xat(1), SLOTS // 2 : SLOTS]
        send(rows, rows, axf_s, ax_r.at[j, 2], dn_x)

    def b_z(j):
        @pl.when(j == 0)
        def _():
            wait(bbuf.at[:, 0, 0, 0, 0:3], bx_r)

        rows = bbuf.at[j, :, c, y, z]
        for p in zs:
            send(rows, rows, bz_s, bz_r.at[j], p)

    def b_y(j):
        wait(bbuf.at[j, :, 0, 0, 0:7], bz_r.at[j])
        rows = bbuf.at[j, :, c, y]
        send(rows, rows, by_s, by_r.at[j, 0], up_y)
        send(rows, rows, by_s, by_r.at[j, 1], dn_y)

    def b_yf(j):
        wait(bbuf.at[j, :, 0, 0], by_r.at[j, 0])
        rows = bbuf.at[j, 0:2, c, yat(-1)]
        send(rows, rows, byf_s, by_r.at[j, 2], up_y)
        wait(bbuf.at[j, :, 0, 0], by_r.at[j, 1])
        rows = bbuf.at[j, 2:4, c, yat(1)]
        send(rows, rows, byf_s, by_r.at[j, 2], dn_y)

    def b_s(j):
        wait(bbuf.at[j, :, 0, 0], by_r.at[j, 2])
        send(bbuf.at[j, :, c], bbuf.at[j, :, c], bs_s, bs_r.at[j], sib)

    def c_y(j):
        @pl.when(j == 0)
        def _():
            wait(cbuf.at[:, 0, 0, 0, 0:3], cx_r)

        rows = cbuf.at[j, :, c, y, z]
        for p in ys:
            send(rows, rows, cy_s, cy_r.at[j], p)

    def c_z(j):
        wait(cbuf.at[j, :, 0, 0, 0:3], cy_r.at[j])
        rows = cbuf.at[j, :, c, :, z]
        send(rows, rows, cz_s, cz_r.at[j, 0], up_z)
        send(rows, rows, cz_s, cz_r.at[j, 1], dn_z)

    def c_hop(j, k):
        block = cbuf.at[j, :, 0, :, 0]
        wait(block, cz_r.at[j, 2 * k - 2])
        rows = cbuf.at[j, :, c, :, zat(-k)]
        send(rows, rows, cz_s, cz_r.at[j, 2 * k], up_z)
        wait(block, cz_r.at[j, 2 * k - 1])
        rows = cbuf.at[j, :, c, :, zat(k)]
        send(rows, rows, cz_s, cz_r.at[j, 2 * k + 1], dn_z)

    def c_last(j):
        block = cbuf.at[j, :, 0, :, 0]
        wait(block, cz_r.at[j, 4])
        rows = cbuf.at[j, 0:2, c, :, zat(-3)]
        send(rows, rows, cz_s, cz_r.at[j, 6], up_z)
        wait(block, cz_r.at[j, 5])
        rows = cbuf.at[j, 2:4, c, :, zat(3)]
        send(rows, rows, cz_s, cz_r.at[j, 6], dn_z)

    def c_s(j):
        wait(cbuf.at[j, :, 0, :, 0], cz_r.at[j, 6])
        send(cbuf.at[j, :, c], cbuf.at[j, :, c], cs_s, cs_r.at[j], sib)

    def w_d(j):
        rows = pl.ds(m8(j * (H // 8), 32), H // 8)
        there = pl.ds(m8(x * H + j * (H // 8), 32), H // 8)
        for d, p in zip((1, 3, 2), xs):
            send(wd.at[rows, pl.ds(m8(xat(d) * DS, 256), DS)], wdv.at[there], ds, dr, p)

    def load(j):
        rows = pl.ds(m8(j * G, 128), G)
        pltpu.make_async_copy(wg.at[rows], wbuf.at[j % 3, :, 0:H], wsem.at[j % 3]).start()
        pltpu.make_async_copy(wu.at[rows], wbuf.at[j % 3, :, H : 2 * H], wsem.at[j % 3]).start()

    def multiply(j):
        wait(slotbuf.at[j, 0], ax_r.at[j, 2])
        wait(bbuf.at[j, :, 0], bs_r.at[j])
        wait(cbuf.at[j, :, 0], cs_r.at[j])
        k = j % 3
        wait(wbuf.at[k], wsem.at[k])
        for q in range(NX):
            total = mm(slotbuf[j, q], wbuf[k, 0:WA])
            rows = mm(sel[q], bbuf[j, q].reshape(PLANE, WB)).astype(BF)
            total = total + mm(rows, wbuf[k, WA : WA + WB])
            rows = mm(sel[q], cbuf[j, q].reshape(PLANE, WC)).astype(BF)
            acc[q] += total + mm(rows, wbuf[k, WA + WB : G])

    stages = (
        (8, multiply), (4, lambda j: c_hop(j, 1)), (3, c_z), (6, load),
        (4, a_x), (4, b_y), (2, b_z), (5, b_yf),
        (6, b_s), (-2, a_z), (2, a_s), (6, c_s),
        (0, a_y), (5, a_xf), (4, lambda j: c_hop(j, 2)), (5, c_last),
        (1, a_yf), (0, c_y),
    )

    @pl.loop(0, N + 8)
    def _(i):
        @pl.when(i < 8)
        def _():
            w_d(i)

        pl.when(i == 0)(routing)
        pl.when(i == 1)(routing_half)
        pl.when(i == 4)(routing_plane)
        pl.when(i == 7)(routing_rest)
        for k, stage in stages:

            @pl.when((i - k >= max(0, -k)) & (i - k < N))
            def _(k=k, stage=stage):
                stage(i - k)

    hot = (iota((128, 2 * 128), 0) == 64 + e).astype(BF)
    for q in range(NX):
        weight = mm(sel[q], mm(meta[q].reshape(PLANE, 128), hot).astype(BF))
        gate, up = acc[q, :, 0:H], acc[q, :, H : 2 * H]
        hbuf[x, q] = (gate / (1.0 + jnp.exp(-gate)) * up * weight).astype(BF)
        for p in xs:
            send(hbuf.at[x, q], hbuf.at[x, q], h_s, h_r.at[q], p)

    cols = NC * NY * NZ * S
    col = iota((128, cols), 1)
    source = col // (NZ * S)
    expert = ((source % NY) * NZ + z) * NC + source // NY
    table = (iota((128, cols), 0) == expert).astype(BF)
    same = iota((NZ * T, cols), 0) // T == (col // S) % NZ
    for q in range(NX):
        found = mm(meta[q, c, y].reshape(NZ * T, 128), table)
        place[q] = jnp.where(same & (found == (col % S + 1).astype(F32)), 1.0, 0.0).astype(BF)

    wait(abuf.at[:, 0, 0, 0:7], az_s)
    wait(abuf.at[:, 0, 0:2], ay_s)
    wait(abuf.at[:, 0, 0:1], ayf_s)
    wait(abuf.at[:, 0], as_s)
    wait(bbuf.at[:, 0, 0, 0, 0:3], bx_s)
    wait(bbuf.at[:, :, 0, 0, 0:7], bz_s)
    wait(bbuf.at[:, 0], by_s)
    wait(bbuf.at[:, 0, 0], byf_s)
    wait(bbuf.at[:, 0:2], bs_s)
    keep.wait()
    wait(wdv.at[0 : 3 * H], dr)

    parts = ((0, 4), (4, 3))

    def o_y(q, h):
        p0, n = parts[h]
        if h == 0:
            wait(hbuf.at[0:3, 0], h_r.at[q])
        total = mm(hbuf[0, q], wdv[0:H, p0 * W2 : (p0 + n) * W2])
        for t in range(1, NX):
            total = total + mm(hbuf[t, q], wdv[t * H : (t + 1) * H, p0 * W2 : (p0 + n) * W2])
        total = total.astype(BF)
        for p in range(n):
            bbuf[p0 + p, q, :, :, 0:2] = total[:, p * W2 : (p + 1) * W2].reshape(NC, NY, 2, T, W2)
            ybuf[q, p0 + p, c * NY + y] = bbuf[p0 + p, q, c, y, 0:2]
        there = ybuf.at[q, p0 : p0 + n, c * NY + y]
        for d in (1, 3, 2):
            for k in (c, 1 - c):
                to = yat(d)
                send(bbuf.at[p0 : p0 + n, q, k, to, 0:2], there, oy_s, oy_r.at[q, h], dev(to, z, k, x))
        send(bbuf.at[p0 : p0 + n, q, 1 - c, y, 0:2], there, oy_s, oy_r.at[q, h], sib)

    def o_z(q, h):
        p0, n = parts[h]
        wait(ybuf.at[q, p0 : p0 + n, 0:7], oy_r.at[q, h])
        for p in range(p0, p0 + n):
            total = mm(place[q], ybuf[q, p].reshape(cols, W2)).astype(BF).reshape(NZ, T, W2)
            abuf[p, 0, q, :, :, 0:W2] = total
            zbuf[q, p, z] = abuf[p, 0, q, z, :, 0:W2]
        for d, dst in zip(zd, zs):
            send(
                abuf.at[p0 : p0 + n, 0, q, zat(d), :, 0:W2], zbuf.at[q, p0 : p0 + n, z],
                oz_s, oz_r.at[q, h], dst,
            )

    def o_x(q, h):
        p0, n = parts[h]
        wait(zbuf.at[q, p0 : p0 + n, 0:7], oz_r.at[q, h])
        for p in range(p0, p0 + n):
            fbuf[q, :, p * W2 : (p + 1) * W2] = jnp.sum(zbuf[q, p].astype(F32), axis=0).astype(BF)
        at = pl.ds(m8(x * DS + p0 * W2, W2), n * W2)
        here_part = fbuf.at[q, :, p0 * W2 : (p0 + n) * W2]

        @pl.when(q == x)
        def _():
            out[:, at] = here_part[...]

        @pl.when(q != x)
        def _():
            send(here_part, out.at[:, at], ox_s, ox_r, dev(y, z, c, q))

    @pl.loop(0, NX + 1)
    def _(q):
        for last, d, h, stage in (
            (0, 0, 0, o_y), (1, 1, 1, o_z), (1, 1, 0, o_x),
            (0, 0, 1, o_y), (0, 0, 0, o_z), (1, 1, 1, o_x),
        ):

            @pl.when((q - d >= 0) & (q - d < NX))
            def _(d=d, h=h, stage=stage):
                stage(q - d, h)

    wait(out.at[:, 0 : 3 * DS], ox_r)
    wait(out.at[:, 0 : 3 * DS], ox_s)
    wait(hbuf.at[0:3], h_s)
    wait(ybuf.at[:, :, 0:7], oy_s)
    wait(zbuf.at[:, :, 0:7], oz_s)
    wait(wdv.at[0 : 3 * H], ds)
    wait(meta.at[0, 0, 0, 0:7], ms.at[0])
    wait(meta.at[0, 0, 0:3], ms.at[1])
    wait(meta.at[0, 0], ms.at[2])
    wait(meta.at[0:3, 0], ms.at[3])
    wait(meta.at[0:3, 0], ms.at[4])
    wait(slotbuf.at[:, 0:2], ax_s)
    wait(slotbuf.at[:, 0:1], axf_s)
    wait(cbuf.at[:, 0, 0, 0, 0:3], cx_s)
    wait(cbuf.at[:, :, 0, 0, 0:3], cy_s)
    wait(cbuf.at[:, :, 0, :, 0:7], cz_s)
    wait(cbuf.at[:, 0:2], cs_s)


def local(tokens, expert_ids, gate_values, w_gate, w_up, w_down):
    vm = pl.BlockSpec(memory_space=pltpu.VMEM)
    hb = pl.BlockSpec(memory_space=pl.ANY)
    dma = pltpu.SemaphoreType.DMA
    return pl.pallas_call(
        layer_kernel,
        out_shape=jax.ShapeDtypeStruct((T, D), BF),
        in_specs=[vm, vm, hb, hb, hb, hb],
        out_specs=vm,
        scratch_shapes=[
            pltpu.VMEM((N, NC, NY, NZ, T, WA), BF),
            pltpu.VMEM((N, NX, SLOTS, WA), BF),
            pltpu.VMEM((N, NX, NC, NY, NZ, T, WB), BF),
            pltpu.VMEM((N, NX, NC, NY, NZ, T, WC), BF),
            pltpu.VMEM((3, G, 2 * H), BF),
            pltpu.VMEM((NX, SLOTS, 2 * H), F32),
            pltpu.VMEM((NX, NC, NY, NZ, T, 128), BF),
            pltpu.VMEM((NX, SLOTS, PLANE), BF),
            pltpu.VMEM((NX * H, DS), BF),
            pltpu.VMEM((NX, NX, SLOTS, H), BF),
            pltpu.VMEM((NX, N2, NC * NY, 2, T, W2), BF),
            pltpu.VMEM((NX, N2, NZ, T, W2), BF),
            pltpu.VMEM((NX, T, DS), BF),
            pltpu.VMEM((NX, NZ * T, NC * NY * NZ * S), BF),
            dma((3,)), dma, dma, dma, dma, dma((5,)), dma((5,)),
            dma, dma((N,)), dma, dma((N, 3)), dma, dma, dma((N,)), dma, dma((N, 3)), dma,
            dma, dma, dma, dma((N,)), dma, dma((N, 3)), dma, dma, dma((N,)),
            dma, dma, dma, dma((N,)), dma, dma((N, 7)), dma, dma((N,)),
            dma, dma((NX,)), dma, dma((NX, 2)), dma, dma((NX, 2)), dma, dma,
        ],
        compiler_params=pltpu.CompilerParams(
            collective_id=0, has_side_effects=True, vmem_limit_bytes=63 << 20
        ),
        name="layer",
    )(expert_ids.T, gate_values.T, tokens, w_gate[0], w_up[0], w_down[0])


def solution(mesh):
    return jax.shard_map(
        local,
        mesh=mesh,
        in_specs=(
            P(("expert", "tensor"), None),
            P(("expert", "tensor"), None),
            P(("expert", "tensor"), None),
            P("expert", None, "tensor"),
            P("expert", None, "tensor"),
            P("expert", "tensor", None),
        ),
        out_specs=P(("expert", "tensor"), None),
        check_vma=False,
    )
```

```python
import jax
import jax.numpy as jnp
from jax import lax
from jax.experimental import pallas as pl
from jax.experimental.pallas import tpu as pltpu
from jax.sharding import PartitionSpec as P

MESH = pl.DeviceIdType.MESH
BF = jnp.bfloat16
F32 = jnp.float32

NX, NY, NZ, NC = 4, 4, 8, 2
T = 16
S = 4
D = 7168
PLANE = NY * NZ * NC * T
SLOTS = NY * NZ * NC * S
WA, WB, WC = 512, 256, 128
G = WA + WB + WC
N = D // G
H = 256
DS = D // NX
W2 = 256
N2 = DS // W2


def here():
    e = lax.axis_index("expert")
    x = lax.axis_index("tensor")
    return e // (NZ * NC), (e // NC) % NZ, e % NC, x, e


def dev(y, z, c, x):
    return ((y * NZ + z) * NC + c, x)


def send(src, dst, ssem, rsem, device):
    pltpu.make_async_remote_copy(
        src_ref=src, dst_ref=dst, send_sem=ssem, recv_sem=rsem, device_id=device, device_id_type=MESH
    ).start()


def wait(ref, sem):
    pltpu.make_async_copy(ref, ref, sem).wait()


def iota(shape, axis):
    return lax.broadcasted_iota(jnp.int32, shape, axis)


def mm(a, b):
    return jnp.dot(a, b, preferred_element_type=F32)


def pick(meta, e):
    hot = (iota((8, 128), 1) == e).astype(BF)
    row = lax.dot_general(hot, meta, (((1,), (1,)), ((), ())), preferred_element_type=F32)[0:1]
    r = iota((SLOTS, PLANE), 0)
    t = iota((SLOTS, PLANE), 1)
    want = (r % S + 1).astype(F32)
    return jnp.where((t // T == r // S) & (row == want), 1.0, 0.0).astype(BF)


def layer_kernel(
    ids, gates, tok, wg, wu, wd, out,
    abuf, slotbuf, bbuf, cbuf, wbuf, acc, meta, sel, wdv, hbuf, ybuf, zbuf, fbuf, place, weight,
    wsem, ds, dr, keep_sem, tsem, ms, mr,
    az_s, az_r, ay_s, ay_r, ayf_s, as_s, as_r, ax_s, ax_r, axf_s,
    bx_s, bx_r, bz_s, bz_r, by_s, by_r, byf_s, bs_s, bs_r,
    cx_s, cx_r, cy_s, cy_r, cz_s, cz_r, cs_s, cs_r,
    h_s, h_r, oy_s, oy_r, oz_s, oz_r, ox_s, ox_r,
):
    y, z, c, x, e = here()
    m8 = pl.multiple_of
    up_y, dn_y = dev((y + 1) % NY, z, c, x), dev((y + NY - 1) % NY, z, c, x)
    up_z, dn_z = dev(y, (z + 1) % NZ, c, x), dev(y, (z + NZ - 1) % NZ, c, x)
    up_x, dn_x = dev(y, z, c, (x + 1) % NX), dev(y, z, c, (x + NX - 1) % NX)
    sib = dev(y, z, 1 - c, x)
    zd = (1, 7, 2, 6, 3, 5, 4)
    xs = [dev(y, z, c, (x + d) % NX) for d in (1, 3, 2)]
    ys = [dev((y + d) % NY, z, c, x) for d in (1, 3, 2)]
    zs = [dev(y, (z + d) % NZ, c, x) for d in zd]
    yat = lambda d: (y + NY + d) % NY
    zat = lambda d: (z + NZ + d) % NZ
    xat = lambda d: (x + NX + d) % NX

    barrier = pltpu.get_barrier_semaphore()
    peers = zs + ys + xs + [sib] + [dev(yat(d), z, 1 - c, x) for d in (1, 3, 2)]
    for p in peers:
        pl.semaphore_signal(barrier, inc=1, device_id=p, device_id_type=MESH)

    for j in range(N):
        at = j * G
        pltpu.make_async_copy(tok.at[:, at : at + WA], abuf.at[j, c, y, z], tsem).start()
        pltpu.make_async_copy(tok.at[:, at + WA : at + WA + WB], bbuf.at[j, x, c, y, z], tsem).start()
        pltpu.make_async_copy(tok.at[:, at + WA + WB : at + G], cbuf.at[j, x, c, y, z], tsem).start()
    mine = pl.ds(m8(x * H, H), H)
    keep = pltpu.make_async_copy(wd.at[:, pl.ds(m8(x * DS, 256), DS)], wdv.at[mine], keep_sem)
    keep.start()

    lane = iota((128, T), 0) % 64
    hit = jnp.zeros((128, T), F32)
    val = jnp.zeros((128, T), F32)
    for k in range(8):
        eq = ids[k : k + 1, :] == lane
        hit = hit + jnp.where(eq, 1.0, 0.0)
        val = val + jnp.where(eq, gates[k : k + 1, :], 0.0)
    before = (iota((T, T), 0) < iota((T, T), 1)).astype(F32)
    rank = mm(hit, before)
    info = jnp.where(iota((128, T), 0) < 64, hit * (rank + 1.0), val).astype(BF)
    eye = (iota((T, T), 0) == iota((T, T), 1)).astype(BF)
    meta[x, c, y, z] = lax.dot_general(
        eye, info, (((1,), (1,)), ((), ())), preferred_element_type=F32
    ).astype(BF)
    acc[...] = jnp.zeros_like(acc)
    wait(tok, tsem)

    pl.semaphore_wait(barrier, len(peers))

    def a_z(j):
        for p in zs:
            send(abuf.at[j, c, y, z], abuf.at[j, c, y, z], az_s, az_r.at[j], p)

    a_z(0)
    for p in zs:
        send(meta.at[x, c, y, z], meta.at[x, c, y, z], ms.at[0], mr.at[0], p)
    for p in xs:
        send(bbuf.at[:, x, c, y, z], bbuf.at[:, x, c, y, z], bx_s, bx_r, p)
    for p in xs:
        send(cbuf.at[:, x, c, y, z], cbuf.at[:, x, c, y, z], cx_s, cx_r, p)
    a_z(1)
    a_z(2)
    a_z(3)
    a_z(4)
    a_z(5)

    def routing():
        wait(meta.at[0, 0, 0, 0:7], mr.at[0])
        for p in ys:
            send(meta.at[x, c, y], meta.at[x, c, y], ms.at[1], mr.at[1], p)

    def routing_half():
        wait(meta.at[0, 0, 0:3], mr.at[1])
        send(meta.at[x, c], meta.at[x, c], ms.at[2], mr.at[2], sib)
        for p in xs:
            send(meta.at[x, c], meta.at[x, c], ms.at[3], mr.at[3], p)

    def routing_plane():
        wait(meta.at[0, 0], mr.at[2])
        sel[x] = pick(meta[x].reshape(PLANE, 128), e)
        wait(meta.at[0:3, 0], mr.at[3])
        for d in (1, 2, 3):
            send(meta.at[xat(d), c], meta.at[xat(d), c], ms.at[4], mr.at[4], sib)

    def routing_rest():
        wait(meta.at[0:3, 0], mr.at[4])
        for d in (1, 2, 3):
            sel[xat(d)] = pick(meta[xat(d)].reshape(PLANE, 128), e)
        hot = (iota((128, 128), 0) == 64 + e).astype(BF)
        for q in range(NX):
            weight[q] = mm(sel[q], mm(meta[q].reshape(PLANE, 128), hot).astype(BF))
        cols = NC * NY * NZ * S
        col = iota((128, cols), 1)
        source = col // (NZ * S)
        expert = ((source % NY) * NZ + z) * NC + source // NY
        table = (iota((128, cols), 0) == expert).astype(BF)
        same = iota((NZ * T, cols), 0) // T == (col // S) % NZ
        for q in range(NX):
            found = mm(meta[q, c, y].reshape(NZ * T, 128), table)
            place[q] = jnp.where(same & (found == (col % S + 1).astype(F32)), 1.0, 0.0).astype(BF)

    def a_y(j):
        wait(abuf.at[j, 0, 0, 0:7], az_r.at[j])
        rows = abuf.at[j, c, y]
        send(rows, rows, ay_s, ay_r.at[j, 0], up_y)
        send(rows, rows, ay_s, ay_r.at[j, 1], dn_y)

    def a_yf(j):
        wait(abuf.at[j, 0, 0], ay_r.at[j, 0])
        rows = abuf.at[j, c, yat(-1), 0:4]
        send(rows, rows, ayf_s, ay_r.at[j, 2], up_y)
        wait(abuf.at[j, 0, 0], ay_r.at[j, 1])
        rows = abuf.at[j, c, yat(1), 4:8]
        send(rows, rows, ayf_s, ay_r.at[j, 2], dn_y)

    def a_s(j):
        wait(abuf.at[j, 0, 0], ay_r.at[j, 2])
        send(abuf.at[j, c], abuf.at[j, c], as_s, as_r.at[j], sib)

    def a_x(j):
        wait(abuf.at[j, 0], as_r.at[j])
        slotbuf[j, x] = mm(sel[x], abuf[j].reshape(PLANE, WA)).astype(BF)
        slots = slotbuf.at[j, x]
        send(slots, slots, ax_s, ax_r.at[j, 0], up_x)
        send(slots, slots, ax_s, ax_r.at[j, 1], dn_x)

    def a_xf(j):
        wait(slotbuf.at[j, 0], ax_r.at[j, 0])
        rows = slotbuf.at[j, xat(-1), 0 : SLOTS // 2]
        send(rows, rows, axf_s, ax_r.at[j, 2], up_x)
        wait(slotbuf.at[j, 0], ax_r.at[j, 1])
        rows = slotbuf.at[j, xat(1), SLOTS // 2 : SLOTS]
        send(rows, rows, axf_s, ax_r.at[j, 2], dn_x)

    def b_z(j):
        @pl.when(j == 0)
        def _():
            wait(bbuf.at[:, 0, 0, 0, 0:3], bx_r)

        rows = bbuf.at[j, :, c, y, z]
        for p in zs:
            send(rows, rows, bz_s, bz_r.at[j], p)

    def b_y(j):
        wait(bbuf.at[j, :, 0, 0, 0:7], bz_r.at[j])
        rows = bbuf.at[j, :, c, y]
        send(rows, rows, by_s, by_r.at[j, 0], up_y)
        send(rows, rows, by_s, by_r.at[j, 1], dn_y)

    def b_yf(j):
        wait(bbuf.at[j, :, 0, 0], by_r.at[j, 0])
        rows = bbuf.at[j, 0:2, c, yat(-1)]
        send(rows, rows, byf_s, by_r.at[j, 2], up_y)
        wait(bbuf.at[j, :, 0, 0], by_r.at[j, 1])
        rows = bbuf.at[j, 2:4, c, yat(1)]
        send(rows, rows, byf_s, by_r.at[j, 2], dn_y)

    def b_s(j):
        wait(bbuf.at[j, :, 0, 0], by_r.at[j, 2])
        send(bbuf.at[j, :, c], bbuf.at[j, :, c], bs_s, bs_r.at[j], sib)

    def c_y(j):
        @pl.when(j == 0)
        def _():
            wait(cbuf.at[:, 0, 0, 0, 0:3], cx_r)

        rows = cbuf.at[j, :, c, y, z]
        for p in ys:
            send(rows, rows, cy_s, cy_r.at[j], p)

    def c_z(j):
        wait(cbuf.at[j, :, 0, 0, 0:3], cy_r.at[j])
        rows = cbuf.at[j, :, c, :, z]
        send(rows, rows, cz_s, cz_r.at[j, 0], up_z)
        send(rows, rows, cz_s, cz_r.at[j, 1], dn_z)

    def c_hop(j, k):
        block = cbuf.at[j, :, 0, :, 0]
        wait(block, cz_r.at[j, 2 * k - 2])
        rows = cbuf.at[j, :, c, :, zat(-k)]
        send(rows, rows, cz_s, cz_r.at[j, 2 * k], up_z)
        wait(block, cz_r.at[j, 2 * k - 1])
        rows = cbuf.at[j, :, c, :, zat(k)]
        send(rows, rows, cz_s, cz_r.at[j, 2 * k + 1], dn_z)

    def c_last(j):
        block = cbuf.at[j, :, 0, :, 0]
        wait(block, cz_r.at[j, 4])
        rows = cbuf.at[j, 0:2, c, :, zat(-3)]
        send(rows, rows, cz_s, cz_r.at[j, 6], up_z)
        wait(block, cz_r.at[j, 5])
        rows = cbuf.at[j, 2:4, c, :, zat(3)]
        send(rows, rows, cz_s, cz_r.at[j, 6], dn_z)

    def c_s(j):
        wait(cbuf.at[j, :, 0, :, 0], cz_r.at[j, 6])
        send(cbuf.at[j, :, c], cbuf.at[j, :, c], cs_s, cs_r.at[j], sib)

    def w_d(j):
        rows = pl.ds(m8(j * (H // 8), 32), H // 8)
        there = pl.ds(m8(x * H + j * (H // 8), 32), H // 8)
        for d, p in zip((1, 3, 2), xs):
            send(wd.at[rows, pl.ds(m8(xat(d) * DS, 256), DS)], wdv.at[there], ds, dr, p)

    def load(j):
        rows = pl.ds(m8(j * G, 128), G)
        pltpu.make_async_copy(wg.at[rows], wbuf.at[j % 3, :, 0:H], wsem.at[j % 3]).start()
        pltpu.make_async_copy(wu.at[rows], wbuf.at[j % 3, :, H : 2 * H], wsem.at[j % 3]).start()

    def multiply_wait(j):
        wait(slotbuf.at[j, 0], ax_r.at[j, 2])
        wait(bbuf.at[j, :, 0], bs_r.at[j])
        wait(cbuf.at[j, :, 0], cs_r.at[j])
        wait(wbuf.at[j % 3], wsem.at[j % 3])

    def product(j, q):
        k = j % 3
        total = mm(slotbuf[j, q], wbuf[k, 0:WA])
        rows = mm(sel[q], bbuf[j, q].reshape(PLANE, WB)).astype(BF)
        total = total + mm(rows, wbuf[k, WA : WA + WB])
        rows = mm(sel[q], cbuf[j, q].reshape(PLANE, WC)).astype(BF)
        return acc[q] + total + mm(rows, wbuf[k, WA + WB : G])

    def multiply(j):
        multiply_wait(j)

        @pl.when(j < N - 1)
        def _():
            for q in range(NX):
                acc[q] = product(j, q)


    stages = (
        (0, a_y), (11, c_s), (10, load), (10, a_xf),
        (5, a_s), (5, b_z), (7, b_y), (6, a_x),
        (12, multiply), (0, c_y), (8, b_yf), (7, lambda j: c_hop(j, 2)),
        (2, a_yf), (10, b_s), (5, lambda j: c_hop(j, 1)), (-6, a_z),
        (8, c_last), (2, c_z),
    )

    @pl.loop(0, N + 12)
    def _(i):
        @pl.when(i < 8)
        def _():
            w_d(i)

        pl.when(i == 0)(routing)
        pl.when(i == 1)(routing_half)
        pl.when(i == 6)(routing_plane)
        pl.when(i == 11)(routing_rest)
        for k, stage in stages:

            @pl.when((i - k >= max(0, -k)) & (i - k < N))
            def _(k=k, stage=stage):
                stage(i - k)

    for q in range(NX):
        total = product(N - 1, q)
        gate, up = total[:, 0:H], total[:, H : 2 * H]
        act = gate / (1.0 + jnp.exp(-gate)) * up
        hbuf[x, q, :, 0:128] = (act[:, 0:128] * weight[q]).astype(BF)
        hbuf[x, q, :, 128:H] = (act[:, 128:H] * weight[q]).astype(BF)
        for p in xs:
            send(hbuf.at[x, q], hbuf.at[x, q], h_s, h_r.at[q], p)

    cols = NC * NY * NZ * S

    wait(abuf.at[:, 0, 0, 0:7], az_s)
    wait(abuf.at[:, 0, 0:2], ay_s)
    wait(abuf.at[:, 0, 0:1], ayf_s)
    wait(abuf.at[:, 0], as_s)
    wait(bbuf.at[:, 0, 0, 0, 0:3], bx_s)
    wait(bbuf.at[:, :, 0, 0, 0:7], bz_s)
    wait(bbuf.at[:, 0], by_s)
    wait(bbuf.at[:, 0, 0], byf_s)
    wait(bbuf.at[:, 0:2], bs_s)
    keep.wait()
    wait(wdv.at[0 : 3 * H], dr)

    parts = ((0, 4), (4, 3))

    def o_y(q, h):
        p0, n = parts[h]
        if h == 0:
            wait(hbuf.at[0:3, 0], h_r.at[q])
        total = mm(hbuf[0, q], wdv[0:H, p0 * W2 : (p0 + n) * W2])
        for t in range(1, NX):
            total = total + mm(hbuf[t, q], wdv[t * H : (t + 1) * H, p0 * W2 : (p0 + n) * W2])
        total = total.astype(BF)
        for p in range(n):
            bbuf[p0 + p, q, :, :, 0:2] = total[:, p * W2 : (p + 1) * W2].reshape(NC, NY, 2, T, W2)
            ybuf[q, p0 + p, c * NY + y] = bbuf[p0 + p, q, c, y, 0:2]
        there = ybuf.at[q, p0 : p0 + n, c * NY + y]
        for d in (1, 3, 2):
            for k in (c, 1 - c):
                to = yat(d)
                send(bbuf.at[p0 : p0 + n, q, k, to, 0:2], there, oy_s, oy_r.at[q, h], dev(to, z, k, x))
        send(bbuf.at[p0 : p0 + n, q, 1 - c, y, 0:2], there, oy_s, oy_r.at[q, h], sib)

    def o_z(q, h):
        p0, n = parts[h]
        wait(ybuf.at[q, p0 : p0 + n, 0:7], oy_r.at[q, h])
        for p in range(p0, p0 + n):
            total = mm(place[q], ybuf[q, p].reshape(cols, W2)).astype(BF).reshape(NZ, T, W2)
            abuf[p, 0, q, :, :, 0:W2] = total
            zbuf[q, p, z] = abuf[p, 0, q, z, :, 0:W2]
        for d, dst in zip(zd, zs):
            send(
                abuf.at[p0 : p0 + n, 0, q, zat(d), :, 0:W2], zbuf.at[q, p0 : p0 + n, z],
                oz_s, oz_r.at[q, h], dst,
            )

    def o_x(q, h):
        p0, n = parts[h]
        wait(zbuf.at[q, p0 : p0 + n, 0:7], oz_r.at[q, h])
        for p in range(p0, p0 + n):
            fbuf[q, :, p * W2 : (p + 1) * W2] = jnp.sum(zbuf[q, p].astype(F32), axis=0).astype(BF)
        at = pl.ds(m8(x * DS + p0 * W2, W2), n * W2)
        here_part = fbuf.at[q, :, p0 * W2 : (p0 + n) * W2]

        @pl.when(q == x)
        def _():
            out[:, at] = here_part[...]

        @pl.when(q != x)
        def _():
            send(here_part, out.at[:, at], ox_s, ox_r, dev(y, z, c, q))

    @pl.loop(0, NX + 1)
    def _(q):
        for last, d, h, stage in (
            (0, 0, 0, o_y), (1, 1, 1, o_z), (1, 1, 0, o_x),
            (0, 0, 1, o_y), (0, 0, 0, o_z), (1, 1, 1, o_x),
        ):

            @pl.when((q - d >= 0) & (q - d < NX))
            def _(d=d, h=h, stage=stage):
                stage(q - d, h)

    wait(out.at[:, 0 : 3 * DS], ox_r)
    wait(out.at[:, 0 : 3 * DS], ox_s)
    wait(hbuf.at[0:3], h_s)
    wait(ybuf.at[:, :, 0:7], oy_s)
    wait(zbuf.at[:, :, 0:7], oz_s)
    wait(wdv.at[0 : 3 * H], ds)
    wait(meta.at[0, 0, 0, 0:7], ms.at[0])
    wait(meta.at[0, 0, 0:3], ms.at[1])
    wait(meta.at[0, 0], ms.at[2])
    wait(meta.at[0:3, 0], ms.at[3])
    wait(meta.at[0:3, 0], ms.at[4])
    wait(slotbuf.at[:, 0:2], ax_s)
    wait(slotbuf.at[:, 0:1], axf_s)
    wait(cbuf.at[:, 0, 0, 0, 0:3], cx_s)
    wait(cbuf.at[:, :, 0, 0, 0:3], cy_s)
    wait(cbuf.at[:, :, 0, :, 0:7], cz_s)
    wait(cbuf.at[:, 0:2], cs_s)


def local(tokens, expert_ids, gate_values, w_gate, w_up, w_down):
    vm = pl.BlockSpec(memory_space=pltpu.VMEM)
    hb = pl.BlockSpec(memory_space=pl.ANY)
    dma = pltpu.SemaphoreType.DMA
    return pl.pallas_call(
        layer_kernel,
        out_shape=jax.ShapeDtypeStruct((T, D), BF),
        in_specs=[vm, vm, hb, hb, hb, hb],
        out_specs=vm,
        scratch_shapes=[
            pltpu.VMEM((N, NC, NY, NZ, T, WA), BF),
            pltpu.VMEM((N, NX, SLOTS, WA), BF),
            pltpu.VMEM((N, NX, NC, NY, NZ, T, WB), BF),
            pltpu.VMEM((N, NX, NC, NY, NZ, T, WC), BF),
            pltpu.VMEM((3, G, 2 * H), BF),
            pltpu.VMEM((NX, SLOTS, 2 * H), F32),
            pltpu.VMEM((NX, NC, NY, NZ, T, 128), BF),
            pltpu.VMEM((NX, SLOTS, PLANE), BF),
            pltpu.VMEM((NX * H, DS), BF),
            pltpu.VMEM((NX, NX, SLOTS, H), BF),
            pltpu.VMEM((NX, N2, NC * NY, 2, T, W2), BF),
            pltpu.VMEM((NX, N2, NZ, T, W2), BF),
            pltpu.VMEM((NX, T, DS), BF),
            pltpu.VMEM((NX, NZ * T, NC * NY * NZ * S), BF),
            pltpu.VMEM((NX, SLOTS, 128), F32),
            dma((3,)), dma, dma, dma, dma, dma((5,)), dma((5,)),
            dma, dma((N,)), dma, dma((N, 3)), dma, dma, dma((N,)), dma, dma((N, 3)), dma,
            dma, dma, dma, dma((N,)), dma, dma((N, 3)), dma, dma, dma((N,)),
            dma, dma, dma, dma((N,)), dma, dma((N, 7)), dma, dma((N,)),
            dma, dma((NX,)), dma, dma((NX, 2)), dma, dma((NX, 2)), dma, dma,
        ],
        compiler_params=pltpu.CompilerParams(
            collective_id=0, has_side_effects=True, vmem_limit_bytes=63 << 20
        ),
        name="layer",
    )(expert_ids.T, gate_values.T, tokens, w_gate[0], w_up[0], w_down[0])


def solution(mesh):
    return jax.shard_map(
        local,
        mesh=mesh,
        in_specs=(
            P(("expert", "tensor"), None),
            P(("expert", "tensor"), None),
            P(("expert", "tensor"), None),
            P("expert", None, "tensor"),
            P("expert", None, "tensor"),
            P("expert", "tensor", None),
        ),
        out_specs=P(("expert", "tensor"), None),
        check_vma=False,
    )
```

```python
import jax
import jax.numpy as jnp
from jax import lax
from jax.experimental import pallas as pl
from jax.experimental.pallas import tpu as pltpu
from jax.sharding import PartitionSpec as P

MESH = pl.DeviceIdType.MESH
BF = jnp.bfloat16
F32 = jnp.float32

NX, NY, NZ, NC = 4, 4, 8, 2
T = 16
S = 4
D = 7168
PLANE = NY * NZ * NC * T
SLOTS = NY * NZ * NC * S
WA, WB, WC = 512, 256, 128
G = WA + WB + WC
N = D // G
H = 256
DS = D // NX
W2 = 256
N2 = DS // W2


def here():
    e = lax.axis_index("expert")
    x = lax.axis_index("tensor")
    return e // (NZ * NC), (e // NC) % NZ, e % NC, x, e


def dev(y, z, c, x):
    return ((y * NZ + z) * NC + c, x)


def send(src, dst, ssem, rsem, device):
    pltpu.make_async_remote_copy(
        src_ref=src, dst_ref=dst, send_sem=ssem, recv_sem=rsem, device_id=device, device_id_type=MESH
    ).start()


def wait(ref, sem):
    pltpu.make_async_copy(ref, ref, sem).wait()


def iota(shape, axis):
    return lax.broadcasted_iota(jnp.int32, shape, axis)


def mm(a, b):
    return jnp.dot(a, b, preferred_element_type=F32)


def pick(meta, e):
    hot = (iota((8, 128), 1) == e).astype(BF)
    row = lax.dot_general(hot, meta, (((1,), (1,)), ((), ())), preferred_element_type=F32)[0:1]
    r = iota((SLOTS, PLANE), 0)
    t = iota((SLOTS, PLANE), 1)
    want = (r % S + 1).astype(F32)
    return jnp.where((t // T == r // S) & (row == want), 1.0, 0.0).astype(BF)


def layer_kernel(
    ids, gates, tok, wg, wu, wd, out,
    abuf, slotbuf, bbuf, cbuf, wbuf, acc, meta, sel, wdv, hbuf, ybuf, zbuf, fbuf, place, weight,
    wsem, ds, dr, keep_sem, tsem, ms, mr,
    az_s, az_r, ay_s, ay_r, ayf_s, as_s, as_r, ax_s, ax_r, axf_s,
    bx_s, bx_r, bz_s, bz_r, by_s, by_r, byf_s, bs_s, bs_r,
    cx_s, cx_r, cy_s, cy_r, cz_s, cz_r, cs_s, cs_r,
    h_s, h_r, oy_s, oy_r, oz_s, oz_r, ox_s, ox_r,
):
    y, z, c, x, e = here()
    m8 = pl.multiple_of
    up_y, dn_y = dev((y + 1) % NY, z, c, x), dev((y + NY - 1) % NY, z, c, x)
    up_z, dn_z = dev(y, (z + 1) % NZ, c, x), dev(y, (z + NZ - 1) % NZ, c, x)
    up_x, dn_x = dev(y, z, c, (x + 1) % NX), dev(y, z, c, (x + NX - 1) % NX)
    sib = dev(y, z, 1 - c, x)
    zd = (1, 7, 2, 6, 3, 5, 4)
    xs = [dev(y, z, c, (x + d) % NX) for d in (1, 3, 2)]
    ys = [dev((y + d) % NY, z, c, x) for d in (1, 3, 2)]
    zs = [dev(y, (z + d) % NZ, c, x) for d in zd]
    yat = lambda d: (y + NY + d) % NY
    zat = lambda d: (z + NZ + d) % NZ
    xat = lambda d: (x + NX + d) % NX

    barrier = pltpu.get_barrier_semaphore()
    peers = zs + ys + xs + [sib] + [dev(yat(d), z, 1 - c, x) for d in (1, 3, 2)]
    for p in peers:
        pl.semaphore_signal(barrier, inc=1, device_id=p, device_id_type=MESH)

    for j in range(N):
        at = j * G
        pltpu.make_async_copy(tok.at[:, at : at + WA], abuf.at[j, c, y, z], tsem).start()
        pltpu.make_async_copy(tok.at[:, at + WA : at + WA + WB], bbuf.at[j, x, c, y, z], tsem).start()
        pltpu.make_async_copy(tok.at[:, at + WA + WB : at + G], cbuf.at[j, x, c, y, z], tsem).start()
    mine = pl.ds(m8(x * H, H), H)
    keep = pltpu.make_async_copy(wd.at[:, pl.ds(m8(x * DS, 256), DS)], wdv.at[mine], keep_sem)
    keep.start()

    lane = iota((128, T), 0) % 64
    hit = jnp.zeros((128, T), F32)
    val = jnp.zeros((128, T), F32)
    for k in range(8):
        eq = ids[k : k + 1, :] == lane
        hit = hit + jnp.where(eq, 1.0, 0.0)
        val = val + jnp.where(eq, gates[k : k + 1, :], 0.0)
    before = (iota((T, T), 0) < iota((T, T), 1)).astype(F32)
    rank = mm(hit, before)
    info = jnp.where(iota((128, T), 0) < 64, hit * (rank + 1.0), val).astype(BF)
    eye = (iota((T, T), 0) == iota((T, T), 1)).astype(BF)
    meta[x, c, y, z] = lax.dot_general(
        eye, info, (((1,), (1,)), ((), ())), preferred_element_type=F32
    ).astype(BF)
    acc[...] = jnp.zeros_like(acc)
    wait(tok, tsem)

    pl.semaphore_wait(barrier, len(peers))

    def a_z(j):
        for p in zs:
            send(abuf.at[j, c, y, z], abuf.at[j, c, y, z], az_s, az_r.at[j], p)

    a_z(0)
    for p in zs:
        send(meta.at[x, c, y, z], meta.at[x, c, y, z], ms.at[0], mr.at[0], p)
    for p in xs:
        send(bbuf.at[:, x, c, y, z], bbuf.at[:, x, c, y, z], bx_s, bx_r, p)
    for p in xs:
        send(cbuf.at[:, x, c, y, z], cbuf.at[:, x, c, y, z], cx_s, cx_r, p)
    a_z(1)
    a_z(2)
    a_z(3)
    a_z(4)
    a_z(5)
    a_z(6)
    a_z(7)

    def routing():
        wait(meta.at[0, 0, 0, 0:7], mr.at[0])
        for p in ys:
            send(meta.at[x, c, y], meta.at[x, c, y], ms.at[1], mr.at[1], p)

    def routing_half():
        wait(meta.at[0, 0, 0:3], mr.at[1])
        send(meta.at[x, c], meta.at[x, c], ms.at[2], mr.at[2], sib)
        for p in xs:
            send(meta.at[x, c], meta.at[x, c], ms.at[3], mr.at[3], p)

    def routing_plane():
        wait(meta.at[0, 0], mr.at[2])
        sel[x] = pick(meta[x].reshape(PLANE, 128), e)
        wait(meta.at[0:3, 0], mr.at[3])
        for d in (1, 2, 3):
            send(meta.at[xat(d), c], meta.at[xat(d), c], ms.at[4], mr.at[4], sib)

    def routing_rest():
        wait(meta.at[0:3, 0], mr.at[4])
        for d in (1, 2, 3):
            sel[xat(d)] = pick(meta[xat(d)].reshape(PLANE, 128), e)
        hot = (iota((128, 128), 0) == 64 + e).astype(BF)
        for q in range(NX):
            weight[q] = mm(sel[q], mm(meta[q].reshape(PLANE, 128), hot).astype(BF))
        cols = NC * NY * NZ * S
        col = iota((128, cols), 1)
        source = col // (NZ * S)
        expert = ((source % NY) * NZ + z) * NC + source // NY
        table = (iota((128, cols), 0) == expert).astype(BF)
        same = iota((NZ * T, cols), 0) // T == (col // S) % NZ
        for q in range(NX):
            found = mm(meta[q, c, y].reshape(NZ * T, 128), table)
            place[q] = jnp.where(same & (found == (col % S + 1).astype(F32)), 1.0, 0.0).astype(BF)

    def a_y(j):
        wait(abuf.at[j, 0, 0, 0:7], az_r.at[j])
        rows = abuf.at[j, c, y]
        send(rows, rows, ay_s, ay_r.at[j, 0], up_y)
        send(rows, rows, ay_s, ay_r.at[j, 1], dn_y)

    def a_yf(j):
        wait(abuf.at[j, 0, 0], ay_r.at[j, 0])
        rows = abuf.at[j, c, yat(-1), 0:4]
        send(rows, rows, ayf_s, ay_r.at[j, 2], up_y)
        wait(abuf.at[j, 0, 0], ay_r.at[j, 1])
        rows = abuf.at[j, c, yat(1), 4:8]
        send(rows, rows, ayf_s, ay_r.at[j, 2], dn_y)

    def a_s(j):
        wait(abuf.at[j, 0, 0], ay_r.at[j, 2])
        send(abuf.at[j, c], abuf.at[j, c], as_s, as_r.at[j], sib)

    def a_x(j):
        wait(abuf.at[j, 0], as_r.at[j])
        slotbuf[j, x] = mm(sel[x], abuf[j].reshape(PLANE, WA)).astype(BF)
        slots = slotbuf.at[j, x]
        send(slots, slots, ax_s, ax_r.at[j, 0], up_x)
        send(slots, slots, ax_s, ax_r.at[j, 1], dn_x)

    def a_xf(j):
        wait(slotbuf.at[j, 0], ax_r.at[j, 0])
        rows = slotbuf.at[j, xat(-1), 0 : SLOTS // 2]
        send(rows, rows, axf_s, ax_r.at[j, 2], up_x)
        wait(slotbuf.at[j, 0], ax_r.at[j, 1])
        rows = slotbuf.at[j, xat(1), SLOTS // 2 : SLOTS]
        send(rows, rows, axf_s, ax_r.at[j, 2], dn_x)

    def b_z(j):
        @pl.when(j == 0)
        def _():
            wait(bbuf.at[:, 0, 0, 0, 0:3], bx_r)

        rows = bbuf.at[j, :, c, y, z]
        for p in zs:
            send(rows, rows, bz_s, bz_r.at[j], p)

    def b_y(j):
        wait(bbuf.at[j, :, 0, 0, 0:7], bz_r.at[j])
        rows = bbuf.at[j, :, c, y]
        send(rows, rows, by_s, by_r.at[j, 0], up_y)
        send(rows, rows, by_s, by_r.at[j, 1], dn_y)

    def b_yf(j):
        wait(bbuf.at[j, :, 0, 0], by_r.at[j, 0])
        rows = bbuf.at[j, 0:2, c, yat(-1)]
        send(rows, rows, byf_s, by_r.at[j, 2], up_y)
        wait(bbuf.at[j, :, 0, 0], by_r.at[j, 1])
        rows = bbuf.at[j, 2:4, c, yat(1)]
        send(rows, rows, byf_s, by_r.at[j, 2], dn_y)

    def b_s(j):
        wait(bbuf.at[j, :, 0, 0], by_r.at[j, 2])
        send(bbuf.at[j, :, c], bbuf.at[j, :, c], bs_s, bs_r.at[j], sib)

    def c_y(j):
        @pl.when(j == 0)
        def _():
            wait(cbuf.at[:, 0, 0, 0, 0:3], cx_r)

        rows = cbuf.at[j, :, c, y, z]
        for p in ys:
            send(rows, rows, cy_s, cy_r.at[j], p)

    def c_z(j):
        wait(cbuf.at[j, :, 0, 0, 0:3], cy_r.at[j])
        rows = cbuf.at[j, :, c, :, z]
        send(rows, rows, cz_s, cz_r.at[j, 0], up_z)
        send(rows, rows, cz_s, cz_r.at[j, 1], dn_z)

    def c_hop(j, k):
        block = cbuf.at[j, :, 0, :, 0]
        wait(block, cz_r.at[j, 2 * k - 2])
        rows = cbuf.at[j, :, c, :, zat(-k)]
        send(rows, rows, cz_s, cz_r.at[j, 2 * k], up_z)
        wait(block, cz_r.at[j, 2 * k - 1])
        rows = cbuf.at[j, :, c, :, zat(k)]
        send(rows, rows, cz_s, cz_r.at[j, 2 * k + 1], dn_z)

    def c_last(j):
        block = cbuf.at[j, :, 0, :, 0]
        wait(block, cz_r.at[j, 4])
        rows = cbuf.at[j, 0:2, c, :, zat(-3)]
        send(rows, rows, cz_s, cz_r.at[j, 6], up_z)
        wait(block, cz_r.at[j, 5])
        rows = cbuf.at[j, 2:4, c, :, zat(3)]
        send(rows, rows, cz_s, cz_r.at[j, 6], dn_z)

    def c_s(j):
        wait(cbuf.at[j, :, 0, :, 0], cz_r.at[j, 6])
        send(cbuf.at[j, :, c], cbuf.at[j, :, c], cs_s, cs_r.at[j], sib)

    def w_d(j):
        rows = pl.ds(m8(j * (H // 8), 32), H // 8)
        there = pl.ds(m8(x * H + j * (H // 8), 32), H // 8)
        for d, p in zip((1, 3, 2), xs):
            send(wd.at[rows, pl.ds(m8(xat(d) * DS, 256), DS)], wdv.at[there], ds, dr, p)

    def load(j):
        rows = pl.ds(m8(j * G, 128), G)
        pltpu.make_async_copy(wg.at[rows], wbuf.at[j % 3, :, 0:H], wsem.at[j % 3]).start()
        pltpu.make_async_copy(wu.at[rows], wbuf.at[j % 3, :, H : 2 * H], wsem.at[j % 3]).start()

    def multiply_wait(j):
        wait(slotbuf.at[j, 0], ax_r.at[j, 2])
        wait(bbuf.at[j, :, 0], bs_r.at[j])
        wait(cbuf.at[j, :, 0], cs_r.at[j])
        wait(wbuf.at[j % 3], wsem.at[j % 3])

    def product(j, q):
        k = j % 3
        total = mm(slotbuf[j, q], wbuf[k, 0:WA])
        rows = mm(sel[q], bbuf[j, q].reshape(PLANE, WB)).astype(BF)
        total = total + mm(rows, wbuf[k, WA : WA + WB])
        rows = mm(sel[q], cbuf[j, q].reshape(PLANE, WC)).astype(BF)
        return acc[q] + total + mm(rows, wbuf[k, WA + WB : G])

    def multiply(j):
        multiply_wait(j)

        @pl.when(j < N - 1)
        def _():
            for q in range(NX):
                acc[q] = product(j, q)


    stages = (
        (4, c_z), (9, a_xf), (3, a_yf), (12, multiply),
        (10, c_s), (6, lambda j: c_hop(j, 1)), (5, a_s), (7, lambda j: c_hop(j, 2)),
        (-8, a_z), (8, c_last), (11, load), (1, c_y),
        (8, b_yf), (5, b_z), (10, b_s), (6, a_x),
        (0, a_y), (6, b_y),
    )

    @pl.loop(0, N + 12)
    def _(i):
        @pl.when(i < 8)
        def _():
            w_d(i)

        pl.when(i == 0)(routing)
        pl.when(i == 1)(routing_half)
        pl.when(i == 6)(routing_plane)
        pl.when(i == 11)(routing_rest)
        for k, stage in stages:

            @pl.when((i - k >= max(0, -k)) & (i - k < N))
            def _(k=k, stage=stage):
                stage(i - k)

    for q in range(NX):
        total = product(N - 1, q)
        gate, up = total[:, 0:H], total[:, H : 2 * H]
        act = gate / (1.0 + jnp.exp(-gate)) * up
        hbuf[x, q, :, 0:128] = (act[:, 0:128] * weight[q]).astype(BF)
        hbuf[x, q, :, 128:H] = (act[:, 128:H] * weight[q]).astype(BF)
        for p in xs:
            send(hbuf.at[x, q], hbuf.at[x, q], h_s, h_r.at[q], p)

    cols = NC * NY * NZ * S

    wait(abuf.at[:, 0, 0, 0:7], az_s)
    wait(abuf.at[:, 0, 0:2], ay_s)
    wait(abuf.at[:, 0, 0:1], ayf_s)
    wait(abuf.at[:, 0], as_s)
    wait(bbuf.at[:, 0, 0, 0, 0:3], bx_s)
    wait(bbuf.at[:, :, 0, 0, 0:7], bz_s)
    wait(bbuf.at[:, 0], by_s)
    wait(bbuf.at[:, 0, 0], byf_s)
    wait(bbuf.at[:, 0:2], bs_s)
    keep.wait()
    wait(wdv.at[0 : 3 * H], dr)

    parts = ((0, 4), (4, 3))

    def o_y(q, h):
        p0, n = parts[h]
        if h == 0:
            wait(hbuf.at[0:3, 0], h_r.at[q])
        total = mm(hbuf[0, q], wdv[0:H, p0 * W2 : (p0 + n) * W2])
        for t in range(1, NX):
            total = total + mm(hbuf[t, q], wdv[t * H : (t + 1) * H, p0 * W2 : (p0 + n) * W2])
        total = total.astype(BF)
        for p in range(n):
            bbuf[p0 + p, q, :, :, 0:2] = total[:, p * W2 : (p + 1) * W2].reshape(NC, NY, 2, T, W2)
            ybuf[q, p0 + p, c * NY + y] = bbuf[p0 + p, q, c, y, 0:2]
        there = ybuf.at[q, p0 : p0 + n, c * NY + y]
        for d in (1, 3, 2):
            for k in (c, 1 - c):
                to = yat(d)
                send(bbuf.at[p0 : p0 + n, q, k, to, 0:2], there, oy_s, oy_r.at[q, h], dev(to, z, k, x))
        send(bbuf.at[p0 : p0 + n, q, 1 - c, y, 0:2], there, oy_s, oy_r.at[q, h], sib)

    def o_z(q, h):
        p0, n = parts[h]
        wait(ybuf.at[q, p0 : p0 + n, 0:7], oy_r.at[q, h])
        for p in range(p0, p0 + n):
            total = mm(place[q], ybuf[q, p].reshape(cols, W2)).astype(BF).reshape(NZ, T, W2)
            abuf[p, 0, q, :, :, 0:W2] = total
            zbuf[q, p, z] = abuf[p, 0, q, z, :, 0:W2]
        for d, dst in zip(zd, zs):
            send(
                abuf.at[p0 : p0 + n, 0, q, zat(d), :, 0:W2], zbuf.at[q, p0 : p0 + n, z],
                oz_s, oz_r.at[q, h], dst,
            )

    def o_x(q, h):
        p0, n = parts[h]
        wait(zbuf.at[q, p0 : p0 + n, 0:7], oz_r.at[q, h])
        for p in range(p0, p0 + n):
            fbuf[q, :, p * W2 : (p + 1) * W2] = jnp.sum(zbuf[q, p].astype(F32), axis=0).astype(BF)
        at = pl.ds(m8(x * DS + p0 * W2, W2), n * W2)
        here_part = fbuf.at[q, :, p0 * W2 : (p0 + n) * W2]

        @pl.when(q == x)
        def _():
            out[:, at] = here_part[...]

        @pl.when(q != x)
        def _():
            send(here_part, out.at[:, at], ox_s, ox_r, dev(y, z, c, q))

    @pl.loop(0, NX + 1)
    def _(q):
        for last, d, h, stage in (
            (0, 0, 0, o_y), (1, 1, 1, o_z), (1, 1, 0, o_x),
            (0, 0, 1, o_y), (0, 0, 0, o_z), (1, 1, 1, o_x),
        ):

            @pl.when((q - d >= 0) & (q - d < NX))
            def _(d=d, h=h, stage=stage):
                stage(q - d, h)

    wait(out.at[:, 0 : 3 * DS], ox_r)
    wait(out.at[:, 0 : 3 * DS], ox_s)
    wait(hbuf.at[0:3], h_s)
    wait(ybuf.at[:, :, 0:7], oy_s)
    wait(zbuf.at[:, :, 0:7], oz_s)
    wait(wdv.at[0 : 3 * H], ds)
    wait(meta.at[0, 0, 0, 0:7], ms.at[0])
    wait(meta.at[0, 0, 0:3], ms.at[1])
    wait(meta.at[0, 0], ms.at[2])
    wait(meta.at[0:3, 0], ms.at[3])
    wait(meta.at[0:3, 0], ms.at[4])
    wait(slotbuf.at[:, 0:2], ax_s)
    wait(slotbuf.at[:, 0:1], axf_s)
    wait(cbuf.at[:, 0, 0, 0, 0:3], cx_s)
    wait(cbuf.at[:, :, 0, 0, 0:3], cy_s)
    wait(cbuf.at[:, :, 0, :, 0:7], cz_s)
    wait(cbuf.at[:, 0:2], cs_s)


def local(tokens, expert_ids, gate_values, w_gate, w_up, w_down):
    vm = pl.BlockSpec(memory_space=pltpu.VMEM)
    hb = pl.BlockSpec(memory_space=pl.ANY)
    dma = pltpu.SemaphoreType.DMA
    return pl.pallas_call(
        layer_kernel,
        out_shape=jax.ShapeDtypeStruct((T, D), BF),
        in_specs=[vm, vm, hb, hb, hb, hb],
        out_specs=vm,
        scratch_shapes=[
            pltpu.VMEM((N, NC, NY, NZ, T, WA), BF),
            pltpu.VMEM((N, NX, SLOTS, WA), BF),
            pltpu.VMEM((N, NX, NC, NY, NZ, T, WB), BF),
            pltpu.VMEM((N, NX, NC, NY, NZ, T, WC), BF),
            pltpu.VMEM((3, G, 2 * H), BF),
            pltpu.VMEM((NX, SLOTS, 2 * H), F32),
            pltpu.VMEM((NX, NC, NY, NZ, T, 128), BF),
            pltpu.VMEM((NX, SLOTS, PLANE), BF),
            pltpu.VMEM((NX * H, DS), BF),
            pltpu.VMEM((NX, NX, SLOTS, H), BF),
            pltpu.VMEM((NX, N2, NC * NY, 2, T, W2), BF),
            pltpu.VMEM((NX, N2, NZ, T, W2), BF),
            pltpu.VMEM((NX, T, DS), BF),
            pltpu.VMEM((NX, NZ * T, NC * NY * NZ * S), BF),
            pltpu.VMEM((NX, SLOTS, 128), F32),
            dma((3,)), dma, dma, dma, dma, dma((5,)), dma((5,)),
            dma, dma((N,)), dma, dma((N, 3)), dma, dma, dma((N,)), dma, dma((N, 3)), dma,
            dma, dma, dma, dma((N,)), dma, dma((N, 3)), dma, dma, dma((N,)),
            dma, dma, dma, dma((N,)), dma, dma((N, 7)), dma, dma((N,)),
            dma, dma((NX,)), dma, dma((NX, 2)), dma, dma((NX, 2)), dma, dma,
        ],
        compiler_params=pltpu.CompilerParams(
            collective_id=0, has_side_effects=True, vmem_limit_bytes=63 << 20
        ),
        name="layer",
    )(expert_ids.T, gate_values.T, tokens, w_gate[0], w_up[0], w_down[0])


def solution(mesh):
    return jax.shard_map(
        local,
        mesh=mesh,
        in_specs=(
            P(("expert", "tensor"), None),
            P(("expert", "tensor"), None),
            P(("expert", "tensor"), None),
            P("expert", None, "tensor"),
            P("expert", None, "tensor"),
            P("expert", "tensor", None),
        ),
        out_specs=P(("expert", "tensor"), None),
        check_vma=False,
    )
```
